32 devices in a mesh: grp: 4 (over x, core), dev: 8 (over z, y).
Axes of the slice: x: 2, y: 2, z: 4, core: 2. Of those that a mesh axis runs over, the one named last changes fastest.
Arguments:
- gradient: bfloat16 [8, 512, 2048], P('grp', 'dev'), may hold values from -400 to 400
- momentum: float32 [32, 512, 512], P(('grp', 'dev')), may hold values from -8 to 8
- master_weight: float32 [32, 512, 512], P(('grp', 'dev')), may hold values from -0.12 to 0.12
- owned_matrix: int32 [4, 2], replicated, may hold values from 0 to 1, each once within a row
- rollout_matrix: int32 [4, 8], P('grp'), may hold values from 0 to 7, each once within a row
Outputs:
- new_momentum: float32 [32, 512, 512], P(('grp', 'dev'))
- update: float32 [32, 512, 512], P(('grp', 'dev'))
- new_master: float32 [32, 512, 512], P(('grp', 'dev'))
- rollout_weight: bfloat16 [32, 512, 2048], P(('grp', 'dev'))
The draws below stay inside these ranges and needn't reach their ends.
Inputs may be any that keep to these rules, and one draw needn't show every extreme that they name: Each row of owned_matrix lists every number 0 to 1 once. Each row of rollout_matrix lists every matrix 0 to 7 once.
All inputs are finite; a program needn't handle non-finite values.
Results may differ from the reference program's by a relative error of at most 0.001.
Values may be sent and summed in bfloat16 or wider, within the bound.
No kernel may reach another device: no remote copies, remote signals or barrier semaphores. Data moves between devices by JAX's collectives and lax.ppermute only.
A program may use at most 64 MiB of HBM per device.

```python
import math
import jax
import jax.numpy as jnp
from jax import lax

ROWS = 512
COLS = 2048
SPLIT = 4
ITERS = 5
SLAB = 512
QUADS = 2
MATS = 8
OWNED = 32
N_GRP = 4


def draw_gradient(key, part):
    first_key, second_key, third_key = jax.random.split(jax.random.fold_in(key, 71), 3)
    base = jnp.clip(jax.random.normal(first_key, (MATS, ROWS, COLS), jnp.float32), -4.0, 4.0)
    top_log = jnp.log(10.0)
    row_scale = jnp.exp(jax.random.uniform(second_key, (MATS, ROWS, 1), jnp.float32, 0.0, 1.0) * top_log)
    col_scale = jnp.exp(jax.random.uniform(third_key, (MATS, 1, COLS), jnp.float32, 0.0, 1.0) * top_log)
    scaled = base * row_scale * col_scale * (100.0 / 256.0)
    return scaled.astype(jnp.bfloat16)


def block_scale(own_key, shape, pieces, smallest, top_value):
    loudness, own = 1.0, jax.random.fold_in(own_key, 6)
    for dim, parts in pieces:
        steps = jnp.exp(jax.random.uniform(jax.random.fold_in(own, dim), (parts,), jnp.float32, smallest / len(pieces), top_value / len(pieces)))
        loudness = loudness * jnp.repeat(steps, shape[dim] // parts).reshape([-1 if axis == dim else 1 for axis in range(len(shape))])
    return loudness


def gaussian(rng, extent, deviation, limit, cuts=(), kind=jnp.bfloat16):
    values = jax.random.normal(rng, extent, jnp.float32) * deviation
    if len(cuts) > 0:
        values = block_scale(rng, extent, cuts, -0.22, 0.18) * values
    return jnp.clip(values, min=-limit, max=limit).astype(kind)


def setup_inputs(seed: int = 0) -> dict:
    key_list = jax.random.split(jax.random.key(seed), 6)
    gradient = draw_gradient(jax.random.fold_in(key_list[5], 71), 0)
    momentum = gaussian(key_list[1], (OWNED, ROWS, SLAB), 3.0, 8.0, ((0, 32),), jnp.float32)
    master_weight = gaussian(key_list[2], (OWNED, ROWS, SLAB), 0.02, 0.12, ((0, 32),), jnp.float32)
    owned_matrix = jax.vmap(lambda own: jax.random.permutation(own, QUADS))(jax.random.split(key_list[3], N_GRP)).reshape((N_GRP, QUADS)).astype(jnp.int32)
    rollout_matrix = jax.vmap(lambda own: jax.random.permutation(own, MATS))(jax.random.split(key_list[4], N_GRP)).reshape((N_GRP, MATS)).astype(jnp.int32)
    return dict(gradient=gradient, momentum=momentum, master_weight=master_weight, owned_matrix=owned_matrix, rollout_matrix=rollout_matrix)


momentum_decay = 0.95
learn_rate = 0.02
weight_decay = 0.1
first_coeff = 3.4445
second_coeff = -4.775
third_coeff = 2.0315
norm_epsilon = 1e-07

def product(left, right):
    return jnp.dot(left, right, precision=lax.Precision.HIGHEST, preferred_element_type=jnp.float32)

def orthogonal(matrix):
    current = matrix * (1.0 / (jnp.sqrt(jnp.sum(matrix * matrix)) + norm_epsilon))
    for step_index in range(ITERS):
        square = product(current, current.T)
        mixed = second_coeff * square + third_coeff * product(square, square)
        current = first_coeff * current + product(mixed, current)
    return current

def reference(gradient, momentum, master_weight, owned_matrix, rollout_matrix):
    groups = owned_matrix.shape[0]
    quads = owned_matrix.shape[1]
    owners = groups * quads
    slab_cols = COLS // SPLIT

    def assemble(slabs):
        return slabs.reshape(owners, SPLIT, ROWS, slab_cols).transpose(0, 2, 1, 3).reshape(owners, ROWS, COLS)

    def split_back(full):
        return full.reshape(owners, ROWS, SPLIT, slab_cols).transpose(0, 2, 1, 3).reshape(owners * SPLIT, ROWS, slab_cols)
    global_id = (jnp.arange(groups, dtype=jnp.int32)[:, None] * quads + owned_matrix.astype(jnp.int32)).reshape(-1)
    chosen = gradient[global_id].astype(jnp.float32)
    moment = assemble(momentum)
    master = assemble(master_weight)
    new_moment = momentum_decay * moment + chosen
    nesterov = chosen + momentum_decay * new_moment
    scale_factor = 0.2 * math.sqrt(max(ROWS, COLS))
    update = lax.map(orthogonal, nesterov) * scale_factor
    new_weight = master - learn_rate * (update + weight_decay * master)
    rounded = new_weight.astype(jnp.bfloat16)
    position = jnp.zeros((owners,), jnp.int32).at[global_id].set(jnp.arange(owners, dtype=jnp.int32))
    rollout = rounded[position[rollout_matrix.reshape(-1).astype(jnp.int32)]]
    return (split_back(new_moment), split_back(update), split_back(new_weight), rollout)
```

```python
import math

import jax
import jax.numpy as jnp
from jax import lax
from jax.sharding import PartitionSpec as P

ITERS = 5
PACK = 4


momentum_decay = 0.95
learn_rate = 0.02
weight_decay = 0.1
first_coeff = 3.4445
second_coeff = -4.775
third_coeff = 2.0315
norm_epsilon = 1e-07


def from_partner(block, axis, bit):
    count = lax.axis_size(axis)
    route = []
    for low in range(count):
        high = low | 1 << bit
        if high != low and high < count:
            route += [(low, high), (high, low)]
    return lax.ppermute(block, axis, route)


def product(left, right, precision=lax.Precision.HIGHEST):
    return jnp.dot(left, right, precision=precision, preferred_element_type=jnp.float32)


def pack_upper(full):
    step = full.shape[0] // PACK
    rows = [full[i * step : (i + 1) * step, i * step :] for i in range(PACK)]
    return [
        jnp.concatenate([rows[0], rows[3]], axis=1),
        jnp.concatenate([rows[1], rows[2]], axis=1),
    ]


def unpack_upper(halves):
    step = halves[0].shape[0]
    rows = [
        halves[0][:, : 4 * step],
        halves[1][:, : 3 * step],
        halves[1][:, 3 * step :],
        halves[0][:, 4 * step :],
    ]

    def block(i, j):
        if i <= j:
            return rows[i][:, (j - i) * step : (j - i + 1) * step]
        return block(j, i).T

    return jnp.concatenate(
        [jnp.concatenate([block(i, j) for j in range(PACK)], axis=1) for i in range(PACK)], axis=0
    )


def gram_sum(slab_part, share_count):
    halves = pack_upper(product(slab_part, slab_part.T))
    bits = list(range(share_count.bit_length() - 1))
    orders = [bits, bits[::-1]]
    for turn in range(len(bits)):
        moved = [from_partner(half, "dev", order[turn]) for half, order in zip(halves, orders)]
        halves = [half + other for half, other in zip(halves, moved)]
    return unpack_upper(halves)


def shards(gradient, momentum, master_weight, owned_matrix, rollout_matrix):
    group = lax.axis_index("grp")
    dev_count = lax.axis_size("dev")
    group_count = lax.axis_size("grp")
    quads = gradient.shape[0]
    row_block = gradient.shape[1]
    columns = gradient.shape[2]
    slab_cols = momentum.shape[2]
    row_count = momentum.shape[1]
    share_count = columns // slab_cols
    all_mats = group_count * quads
    slot_count = all_mats // dev_count
    mine = lax.dynamic_index_in_dim(owned_matrix, group, 0, keepdims=False)
    local_ids = jnp.arange(quads, dtype=jnp.int32)
    picker = (mine[:, None] == local_ids[None, :]).astype(jnp.bfloat16)
    ordered = jnp.einsum(
        "qm,mrc->rqc", picker, gradient, preferred_element_type=jnp.float32
    ).astype(jnp.bfloat16)
    arrived = lax.all_to_all(
        ordered.reshape(row_block, dev_count, slab_cols),
        "dev",
        split_axis=1,
        concat_axis=0,
        tiled=True,
    )
    grad_slab = arrived.reshape(row_count, slab_cols).astype(jnp.float32)
    new_moment = momentum_decay * momentum[0] + grad_slab
    nesterov = grad_slab + momentum_decay * new_moment
    gram = gram_sum(nesterov, share_count)
    norm_sq = jnp.trace(gram)
    factor = 1.0 / (jnp.sqrt(norm_sq) + norm_epsilon)
    current = nesterov * factor
    square = gram * (factor * factor)
    for step_index in range(ITERS):
        mixed = second_coeff * square + third_coeff * product(square, square)
        current = first_coeff * current + product(mixed, current)
        if step_index < ITERS - 1:
            half_way = first_coeff * square + product(mixed, square)
            square = first_coeff * half_way + product(half_way, mixed)
    scale_factor = 0.2 * math.sqrt(max(row_count, columns))
    update = current * scale_factor
    master = master_weight[0]
    new_weight = master - learn_rate * (update + weight_decay * master)
    rounded = new_weight.astype(jnp.bfloat16)
    own_rows = lax.all_to_all(
        rounded.reshape(dev_count, row_block, slab_cols),
        "dev",
        split_axis=0,
        concat_axis=2,
        tiled=True,
    )
    copies = lax.all_gather(own_rows, "grp", axis=0, tiled=True)
    blocks = copies.reshape(group_count, row_block, quads, columns)
    owner_ids = jnp.arange(quads, dtype=jnp.int32)
    inverse = jnp.sum(
        jnp.where(
            owned_matrix[:, :, None] == local_ids[None, None, :], owner_ids[None, :, None], 0
        ),
        axis=1,
    )
    inverse_flat = inverse.reshape(-1)
    targets = rollout_matrix[0]
    global_ids = jnp.arange(all_mats, dtype=jnp.int32)
    target_group = targets // quads
    target_owner = jnp.sum(
        jnp.where(targets[:, None] == global_ids[None, :], inverse_flat[None, :], 0), axis=1
    )
    flat_owner = target_group * quads + target_owner
    chooser = (
        (flat_owner[:, None] == global_ids[None, :])
        .astype(jnp.bfloat16)
        .reshape(all_mats, group_count, quads)
    )
    outgoing = jnp.einsum(
        "pgq,grqc->prc", chooser, blocks, preferred_element_type=jnp.float32
    ).astype(jnp.bfloat16)
    landed = lax.all_to_all(
        outgoing.reshape(dev_count, slot_count, row_block, columns),
        "dev",
        split_axis=0,
        concat_axis=2,
        tiled=True,
    )
    rollout = landed.reshape(slot_count, row_count, columns)
    return (new_moment[None], update[None], new_weight[None], rollout)


def solution(mesh):
    placed = (
        P("grp", "dev", None),
        P(("grp", "dev"), None, None),
        P(("grp", "dev"), None, None),
        P(),
        P("grp", None),
    )
    return jax.shard_map(
        shards,
        mesh=mesh,
        in_specs=placed,
        out_specs=(
            P(("grp", "dev"), None, None),
            P(("grp", "dev"), None, None),
            P(("grp", "dev"), None, None),
            P(("grp", "dev"), None, None),
        ),
        check_vma=False,
    )
```

```python
import functools
import math

import jax
import jax.numpy as jnp
from jax import lax
from jax.experimental import pallas as pl
from jax.experimental.pallas import tpu as pltpu
from jax.sharding import PartitionSpec as P

ITERS = 5
PACK = 4


momentum_decay = 0.95
learn_rate = 0.02
weight_decay = 0.1
first_coeff = 3.4445
second_coeff = -4.775
third_coeff = 2.0315
norm_epsilon = 1e-07


def from_partner(block, axis, bit):
    count = lax.axis_size(axis)
    route = []
    for low in range(count):
        high = low | 1 << bit
        if high != low and high < count:
            route += [(low, high), (high, low)]
    return lax.ppermute(block, axis, route)


def product(left, right, precision=lax.Precision.HIGHEST):
    return jnp.dot(left, right, precision=precision, preferred_element_type=jnp.float32)


def pack_upper(full):
    step = full.shape[0] // PACK
    rows = [full[i * step : (i + 1) * step, i * step :] for i in range(PACK)]
    return [
        jnp.concatenate([rows[0], rows[3]], axis=1),
        jnp.concatenate([rows[1], rows[2]], axis=1),
    ]


def unpack_upper(halves):
    step = halves[0].shape[0]
    rows = [
        halves[0][:, : 4 * step],
        halves[1][:, : 3 * step],
        halves[1][:, 3 * step :],
        halves[0][:, 4 * step :],
    ]

    def block(i, j):
        if i <= j:
            return rows[i][:, (j - i) * step : (j - i + 1) * step]
        return block(j, i).T

    return jnp.concatenate(
        [jnp.concatenate([block(i, j) for j in range(PACK)], axis=1) for i in range(PACK)], axis=0
    )


def gram_sum(slab_part, share_count):
    halves = pack_upper(product(slab_part, slab_part.T))
    bits = list(range(share_count.bit_length() - 1))
    orders = [bits, bits[::-1]]
    for turn in range(len(bits)):
        moved = [from_partner(half, "dev", order[turn]) for half, order in zip(halves, orders)]
        halves = [half + other for half, other in zip(halves, moved)]
    return unpack_upper(halves)


def flipped(block, axis, flip):
    return lax.ppermute(block, axis, [(i, i ^ flip) for i in range(lax.axis_size(axis))])


def choose(items, index):
    bit = 0
    while len(items) > 1:
        odd = (index >> bit) & 1 == 1
        items = [jnp.where(odd, items[i + 1], items[i]) for i in range(0, len(items), 2)]
        bit += 1
    return items[0]


def owner_of(owned_matrix, quads):
    ids = jnp.arange(quads, dtype=jnp.int32)
    return jnp.sum(
        jnp.where(owned_matrix[:, :, None] == ids[None, None, :], ids[None, :, None], 0), axis=1
    ).reshape(-1)


def wanted_slots(rollout_matrix, owned_matrix, share_count):
    quads = owned_matrix.shape[1]
    group = lax.axis_index("grp")
    place = lax.axis_index("dev")
    inverse = owner_of(owned_matrix, quads)
    mats = jnp.arange(inverse.shape[0], dtype=jnp.int32)
    targets = rollout_matrix[0]
    owner = jnp.sum(jnp.where(targets[:, None] == mats[None, :], inverse[None, :], 0), axis=1)
    slot = ((targets // quads) ^ group) * quads + (owner ^ (place // share_count))
    return [
        lax.dynamic_index_in_dim(slot, place ^ turn, 0, keepdims=False)
        for turn in range(share_count)
    ]


def lay_kernel(share_count, *refs):
    mine = lax.axis_index("dev") % share_count
    blocks, out, done = refs[:share_count], refs[-2], refs[-1]
    cols = blocks[0].shape[1]
    moves = []
    for turn, block in enumerate(blocks):
        start = pl.multiple_of((mine ^ turn) * cols, cols)
        moves.append(
            pltpu.make_async_copy(block, out.at[:, pl.ds(start, cols)], done.at[turn])
        )
    for move in moves:
        move.start()
    for move in moves:
        move.wait()


def lay(blocks):
    share_count = len(blocks)
    rows, cols = blocks[0].shape
    return pl.pallas_call(
        functools.partial(lay_kernel, share_count),
        out_shape=jax.ShapeDtypeStruct((rows, cols * share_count), blocks[0].dtype),
        in_specs=[pl.BlockSpec(memory_space=pltpu.VMEM)] * share_count,
        out_specs=pl.BlockSpec(memory_space=pltpu.HBM),
        scratch_shapes=[pltpu.SemaphoreType.DMA((share_count,))],
    )(*blocks)


def sync_two_halves(rounded, slots, share_count):
    group_count = lax.axis_size("grp")
    tables = []
    for start in (rounded, flipped(rounded, "dev", share_count)):
        table = {0: start}
        for bit in range(group_count.bit_length() - 2, -1, -1):
            for key in list(table):
                table[key | 1 << bit] = flipped(table[key], "grp", 1 << bit)
        tables.append(table)
    slabs = [table[key] for key in range(group_count) for table in tables]
    picked = [choose(slabs, slot) for slot in slots]
    return lay(
        [picked[0]] + [flipped(picked[turn], "dev", turn) for turn in range(1, share_count)]
    )


def sync_any(rounded, rollout_matrix, owned_matrix, row_block, columns):
    dev_count = lax.axis_size("dev")
    group_count = lax.axis_size("grp")
    quads = owned_matrix.shape[1]
    row_count, slab_cols = rounded.shape
    all_mats = group_count * quads
    slot_count = all_mats // dev_count
    own_rows = lax.all_to_all(
        rounded.reshape(dev_count, row_block, slab_cols),
        "dev",
        split_axis=0,
        concat_axis=2,
        tiled=True,
    )
    copies = lax.all_gather(own_rows, "grp", axis=0, tiled=True)
    blocks = copies.reshape(group_count, row_block, quads, columns)
    inverse_flat = owner_of(owned_matrix, quads)
    targets = rollout_matrix[0]
    global_ids = jnp.arange(all_mats, dtype=jnp.int32)
    target_group = targets // quads
    target_owner = jnp.sum(
        jnp.where(targets[:, None] == global_ids[None, :], inverse_flat[None, :], 0), axis=1
    )
    flat_owner = target_group * quads + target_owner
    chooser = (
        (flat_owner[:, None] == global_ids[None, :])
        .astype(jnp.bfloat16)
        .reshape(all_mats, group_count, quads)
    )
    outgoing = jnp.einsum(
        "pgq,grqc->prc", chooser, blocks, preferred_element_type=jnp.float32
    ).astype(jnp.bfloat16)
    landed = lax.all_to_all(
        outgoing.reshape(dev_count, slot_count, row_block, columns),
        "dev",
        split_axis=0,
        concat_axis=2,
        tiled=True,
    )
    return landed.reshape(slot_count, row_count, columns)


def shards(gradient, momentum, master_weight, owned_matrix, rollout_matrix):
    group = lax.axis_index("grp")
    dev_count = lax.axis_size("dev")
    group_count = lax.axis_size("grp")
    quads = gradient.shape[0]
    row_block = gradient.shape[1]
    columns = gradient.shape[2]
    slab_cols = momentum.shape[2]
    row_count = momentum.shape[1]
    share_count = columns // slab_cols
    two_halves = (
        quads == 2
        and dev_count == quads * share_count
        and not share_count & (share_count - 1)
        and not group_count & (group_count - 1)
    )
    mine = lax.dynamic_index_in_dim(owned_matrix, group, 0, keepdims=False)
    local_ids = jnp.arange(quads, dtype=jnp.int32)
    picker = (mine[:, None] == local_ids[None, :]).astype(jnp.bfloat16)
    ordered = jnp.einsum(
        "qm,mrc->rqc", picker, gradient, preferred_element_type=jnp.float32
    ).astype(jnp.bfloat16)
    arrived = lax.all_to_all(
        ordered.reshape(row_block, dev_count, slab_cols),
        "dev",
        split_axis=1,
        concat_axis=0,
        tiled=True,
    )
    grad_slab = arrived.reshape(row_count, slab_cols).astype(jnp.float32)
    new_moment = momentum_decay * momentum[0] + grad_slab
    nesterov = grad_slab + momentum_decay * new_moment
    if two_halves:
        slots = wanted_slots(rollout_matrix, owned_matrix, share_count)
        nesterov, slots = lax.optimization_barrier((nesterov, slots))
    gram = gram_sum(nesterov, share_count)
    norm_sq = jnp.trace(gram)
    factor = 1.0 / (jnp.sqrt(norm_sq) + norm_epsilon)
    current = nesterov * factor
    square = gram * (factor * factor)
    for step_index in range(ITERS):
        mixed = second_coeff * square + third_coeff * product(square, square)
        current = first_coeff * current + product(mixed, current)
        if step_index < ITERS - 1:
            half_way = first_coeff * square + product(mixed, square)
            square = first_coeff * half_way + product(half_way, mixed)
    scale_factor = 0.2 * math.sqrt(max(row_count, columns))
    update = current * scale_factor
    master = master_weight[0]
    new_weight = master - learn_rate * (update + weight_decay * master)
    rounded = new_weight.astype(jnp.bfloat16)
    if two_halves:
        rollout = sync_two_halves(rounded, slots, share_count)[None]
    else:
        rollout = sync_any(rounded, rollout_matrix, owned_matrix, row_block, columns)
    return (new_moment[None], update[None], new_weight[None], rollout)


def solution(mesh):
    placed = (
        P("grp", "dev", None),
        P(("grp", "dev"), None, None),
        P(("grp", "dev"), None, None),
        P(),
        P("grp", None),
    )
    return jax.shard_map(
        shards,
        mesh=mesh,
        in_specs=placed,
        out_specs=(
            P(("grp", "dev"), None, None),
            P(("grp", "dev"), None, None),
            P(("grp", "dev"), None, None),
            P(("grp", "dev"), None, None),
        ),
        check_vma=False,
    )
```

```python
import functools
import math

import jax
import jax.numpy as jnp
from jax import lax
from jax.experimental import pallas as pl
from jax.experimental.pallas import tpu as pltpu
from jax.sharding import PartitionSpec as P

ITERS = 5
PACK = 4


momentum_decay = 0.95
learn_rate = 0.02
weight_decay = 0.1
first_coeff = 3.4445
second_coeff = -4.775
third_coeff = 2.0315
norm_epsilon = 1e-07


def from_partner(block, axis, bit):
    count = lax.axis_size(axis)
    route = []
    for low in range(count):
        high = low | 1 << bit
        if high != low and high < count:
            route += [(low, high), (high, low)]
    return lax.ppermute(block, axis, route)


def product(left, right, precision=lax.Precision.HIGHEST):
    return jnp.dot(left, right, precision=precision, preferred_element_type=jnp.float32)


def pack_upper(full):
    step = full.shape[0] // PACK
    rows = [full[i * step : (i + 1) * step, i * step :] for i in range(PACK)]
    return [
        jnp.concatenate([rows[0], rows[3]], axis=1),
        jnp.concatenate([rows[1], rows[2]], axis=1),
    ]


def gram_sum(slab_part, share_count):
    halves = pack_upper(product(slab_part, slab_part.T))
    moved = [jnp.zeros_like(half) for half in halves]
    bits = list(range(share_count.bit_length() - 1))
    orders = [bits, bits[::-1]]
    for turn in range(len(bits)):
        halves = [half + other for half, other in zip(halves, moved)] if turn else halves
        moved = [from_partner(half, "dev", order[turn]) for half, order in zip(halves, orders)]
    return halves, moved


def parts_of(value, count):
    parts = []
    for _ in range(count - 1):
        high = value.astype(jnp.bfloat16)
        parts.append(high)
        value = value - high.astype(jnp.float32)
    return parts + [value.astype(jnp.bfloat16)]


def split_product(left, right):
    count = len(left)
    total = None
    for order in range(count - 1, -1, -1):
        for i in range(order + 1):
            term = jnp.dot(left[i], right[order - i], preferred_element_type=jnp.float32)
            total = term if total is None else total + term
    return total


def newton_kernel(iters, scale, a0, a1, b0, b1, p_ref, w_ref, u_ref, n_ref, r_ref, gram, cur):
    rows = gram.shape[0]
    step = rows // PACK
    halves = [a0[...] + a1[...], b0[...] + b1[...]]
    bands = [
        halves[0][:, : 4 * step],
        halves[1][:, : 3 * step],
        halves[1][:, 3 * step :],
        halves[0][:, 4 * step :],
    ]
    eye = lax.broadcasted_iota(jnp.int32, (step, step), 0) == lax.broadcasted_iota(
        jnp.int32, (step, step), 1
    )
    diag = sum(jnp.where(eye, band[:, :step], 0.0) for band in bands)
    norm_sq = jnp.sum(jnp.sum(diag, axis=1, keepdims=True), axis=0, keepdims=True)
    factor = 1.0 / (jnp.sqrt(norm_sq) + norm_epsilon)
    square = factor * factor
    for i, band in enumerate(bands):
        scaled = band * square
        gram[i * step : (i + 1) * step, i * step :] = scaled
        for j in range(i + 1, PACK):
            gram[j * step : (j + 1) * step, i * step : (i + 1) * step] = scaled[
                :, (j - i) * step : (j - i + 1) * step
            ].T
    cur[...] = p_ref[...] * factor

    def mixed_of(a, a_parts):
        return second_coeff * a + third_coeff * split_product(a_parts[:2], a_parts[:2])

    def apply(mixed_parts):
        x = cur[...]
        return first_coeff * x + split_product(mixed_parts[:2], parts_of(x, 2))

    def advance(count):
        a = gram[...]
        a_parts = parts_of(a, count)
        mixed_parts = parts_of(mixed_of(a, a_parts if count == 2 else parts_of(a, 2)), count)
        half_way = first_coeff * a + split_product(mixed_parts, a_parts)
        gram[...] = first_coeff * half_way + split_product(parts_of(half_way, count), mixed_parts)
        cur[...] = apply(mixed_parts)

    advance(3)
    if iters > 2:
        lax.fori_loop(1, iters - 1, lambda _, none: (advance(2), none)[1], 0)
    a = gram[...]
    u = apply(parts_of(mixed_of(a, parts_of(a, 2)), 2)) * scale
    w = w_ref[...]
    new = w - learn_rate * (u + weight_decay * w)
    r_ref[...] = new.astype(r_ref.dtype)
    u_ref[...] = u
    n_ref[...] = new


def newton(halves, moved, nesterov, master, iters, scale):
    rows, cols = nesterov.shape
    vmem = pl.BlockSpec(memory_space=pltpu.VMEM)
    f32 = jax.ShapeDtypeStruct((rows, cols), jnp.float32)
    return pl.pallas_call(
        functools.partial(newton_kernel, iters, scale),
        out_shape=[f32, f32, jax.ShapeDtypeStruct((rows, cols), jnp.bfloat16)],
        in_specs=[vmem] * 6,
        out_specs=[vmem] * 3,
        scratch_shapes=[pltpu.VMEM((rows, rows), jnp.float32), pltpu.VMEM((rows, cols), jnp.float32)],
        cost_estimate=pl.CostEstimate(
            flops=2 * 60 * rows * rows * cols, bytes_accessed=24 * rows * cols, transcendentals=0
        ),
        compiler_params=pltpu.CompilerParams(vmem_limit_bytes=40 << 20),
    )(halves[0], moved[0], halves[1], moved[1], nesterov, master)


def flipped(block, axis, flip):
    return lax.ppermute(block, axis, [(i, i ^ flip) for i in range(lax.axis_size(axis))])


def choose(items, index):
    bit = 0
    while len(items) > 1:
        odd = (index >> bit) & 1 == 1
        items = [jnp.where(odd, items[i + 1], items[i]) for i in range(0, len(items), 2)]
        bit += 1
    return items[0]


def owner_of(owned_matrix, quads):
    ids = jnp.arange(quads, dtype=jnp.int32)
    return jnp.sum(
        jnp.where(owned_matrix[:, :, None] == ids[None, None, :], ids[None, :, None], 0), axis=1
    ).reshape(-1)


def wanted_slots(rollout_matrix, owned_matrix, share_count):
    quads = owned_matrix.shape[1]
    group = lax.axis_index("grp")
    place = lax.axis_index("dev")
    inverse = owner_of(owned_matrix, quads)
    mats = jnp.arange(inverse.shape[0], dtype=jnp.int32)
    targets = rollout_matrix[0]
    owner = jnp.sum(jnp.where(targets[:, None] == mats[None, :], inverse[None, :], 0), axis=1)
    slot = ((targets // quads) ^ group) * quads + (owner ^ (place // share_count))
    return [
        lax.dynamic_index_in_dim(slot, place ^ turn, 0, keepdims=False)
        for turn in range(share_count)
    ]


def lay_kernel(share_count, *refs):
    mine = lax.axis_index("dev") % share_count
    blocks, out, done = refs[:share_count], refs[-2], refs[-1]
    cols = blocks[0].shape[1]
    moves = []
    for turn, block in enumerate(blocks):
        start = pl.multiple_of((mine ^ turn) * cols, cols)
        moves.append(
            pltpu.make_async_copy(block, out.at[:, pl.ds(start, cols)], done.at[turn])
        )
    for move in moves:
        move.start()
    for move in moves:
        move.wait()


def lay(blocks):
    share_count = len(blocks)
    rows, cols = blocks[0].shape
    return pl.pallas_call(
        functools.partial(lay_kernel, share_count),
        out_shape=jax.ShapeDtypeStruct((rows, cols * share_count), blocks[0].dtype),
        in_specs=[pl.BlockSpec(memory_space=pltpu.VMEM)] * share_count,
        out_specs=pl.BlockSpec(memory_space=pltpu.HBM),
        scratch_shapes=[pltpu.SemaphoreType.DMA((share_count,))],
    )(*blocks)


def sync_two_halves(rounded, slots, share_count):
    group_count = lax.axis_size("grp")
    tables = []
    for start in (rounded, flipped(rounded, "dev", share_count)):
        table = {0: start}
        for bit in range(group_count.bit_length() - 2, -1, -1):
            for key in list(table):
                table[key | 1 << bit] = flipped(table[key], "grp", 1 << bit)
        tables.append(table)
    slabs = [table[key] for key in range(group_count) for table in tables]
    picked = [choose(slabs, slot) for slot in slots]
    return lay(
        [picked[0]] + [flipped(picked[turn], "dev", turn) for turn in range(1, share_count)]
    )


def sync_any(rounded, rollout_matrix, owned_matrix, row_block, columns):
    dev_count = lax.axis_size("dev")
    group_count = lax.axis_size("grp")
    quads = owned_matrix.shape[1]
    row_count, slab_cols = rounded.shape
    all_mats = group_count * quads
    slot_count = all_mats // dev_count
    own_rows = lax.all_to_all(
        rounded.reshape(dev_count, row_block, slab_cols),
        "dev",
        split_axis=0,
        concat_axis=2,
        tiled=True,
    )
    copies = lax.all_gather(own_rows, "grp", axis=0, tiled=True)
    blocks = copies.reshape(group_count, row_block, quads, columns)
    inverse_flat = owner_of(owned_matrix, quads)
    targets = rollout_matrix[0]
    global_ids = jnp.arange(all_mats, dtype=jnp.int32)
    target_group = targets // quads
    target_owner = jnp.sum(
        jnp.where(targets[:, None] == global_ids[None, :], inverse_flat[None, :], 0), axis=1
    )
    flat_owner = target_group * quads + target_owner
    chooser = (
        (flat_owner[:, None] == global_ids[None, :])
        .astype(jnp.bfloat16)
        .reshape(all_mats, group_count, quads)
    )
    outgoing = jnp.einsum(
        "pgq,grqc->prc", chooser, blocks, preferred_element_type=jnp.float32
    ).astype(jnp.bfloat16)
    landed = lax.all_to_all(
        outgoing.reshape(dev_count, slot_count, row_block, columns),
        "dev",
        split_axis=0,
        concat_axis=2,
        tiled=True,
    )
    return landed.reshape(slot_count, row_count, columns)


def shards(gradient, momentum, master_weight, owned_matrix, rollout_matrix):
    group = lax.axis_index("grp")
    dev_count = lax.axis_size("dev")
    group_count = lax.axis_size("grp")
    quads = gradient.shape[0]
    row_block = gradient.shape[1]
    columns = gradient.shape[2]
    slab_cols = momentum.shape[2]
    row_count = momentum.shape[1]
    share_count = columns // slab_cols
    two_halves = (
        quads == 2
        and dev_count == quads * share_count
        and not share_count & (share_count - 1)
        and not group_count & (group_count - 1)
    )
    mine = lax.dynamic_index_in_dim(owned_matrix, group, 0, keepdims=False)
    local_ids = jnp.arange(quads, dtype=jnp.int32)
    picker = (mine[:, None] == local_ids[None, :]).astype(jnp.bfloat16)
    ordered = jnp.einsum(
        "qm,mrc->rqc", picker, gradient, preferred_element_type=jnp.float32
    ).astype(jnp.bfloat16)
    arrived = lax.all_to_all(
        ordered.reshape(row_block, dev_count, slab_cols),
        "dev",
        split_axis=1,
        concat_axis=0,
        tiled=True,
    )
    grad_slab = arrived.reshape(row_count, slab_cols).astype(jnp.float32)
    new_moment = momentum_decay * momentum[0] + grad_slab
    nesterov = grad_slab + momentum_decay * new_moment
    if two_halves:
        slots = wanted_slots(rollout_matrix, owned_matrix, share_count)
        nesterov, slots = lax.optimization_barrier((nesterov, slots))
    halves, moved = gram_sum(nesterov, share_count)
    scale_factor = 0.2 * math.sqrt(max(row_count, columns))
    update, new_weight, rounded = newton(
        halves, moved, nesterov, master_weight[0], ITERS, scale_factor
    )
    if two_halves:
        rollout = sync_two_halves(rounded, slots, share_count)[None]
    else:
        rollout = sync_any(rounded, rollout_matrix, owned_matrix, row_block, columns)
    return (new_moment[None], update[None], new_weight[None], rollout)


def solution(mesh):
    placed = (
        P("grp", "dev", None),
        P(("grp", "dev"), None, None),
        P(("grp", "dev"), None, None),
        P(),
        P("grp", None),
    )
    return jax.shard_map(
        shards,
        mesh=mesh,
        in_specs=placed,
        out_specs=(
            P(("grp", "dev"), None, None),
            P(("grp", "dev"), None, None),
            P(("grp", "dev"), None, None),
            P(("grp", "dev"), None, None),
        ),
        check_vma=False,
    )
```

```python
import functools
import math

import jax
import jax.numpy as jnp
from jax import lax
from jax.experimental import pallas as pl
from jax.experimental.pallas import tpu as pltpu
from jax.sharding import PartitionSpec as P


ITERS = 5
PACK = 4
CHUNKS = 2


momentum_decay = 0.95
learn_rate = 0.02
weight_decay = 0.1
first_coeff = 3.4445
second_coeff = -4.775
third_coeff = 2.0315
norm_epsilon = 1e-07


def from_partner(block, axis, bit):
    count = lax.axis_size(axis)
    route = []
    for low in range(count):
        high = low | 1 << bit
        if high != low and high < count:
            route += [(low, high), (high, low)]
    return lax.ppermute(block, axis, route)


def product(left, right, precision=lax.Precision.HIGHEST):
    return jnp.dot(left, right, precision=precision, preferred_element_type=jnp.float32)


def pack_upper(full):
    step = full.shape[0] // PACK
    rows = [full[i * step : (i + 1) * step, i * step :] for i in range(PACK)]
    return [
        jnp.concatenate([rows[0], rows[3]], axis=1),
        jnp.concatenate([rows[1], rows[2]], axis=1),
    ]


def gram_sum(slab_part, share_count):
    halves = pack_upper(product(slab_part, slab_part.T))
    moved = [jnp.zeros_like(half) for half in halves]
    bits = list(range(share_count.bit_length() - 1))
    orders = [bits, bits[::-1]]
    for turn in range(len(bits)):
        halves = [half + other for half, other in zip(halves, moved)] if turn else halves
        moved = [from_partner(half, "dev", order[turn]) for half, order in zip(halves, orders)]
    return halves, moved


def parts_of(value, count):
    parts = []
    for _ in range(count - 1):
        high = value.astype(jnp.bfloat16)
        parts.append(high)
        value = value - high.astype(jnp.float32)
    return parts + [value.astype(jnp.bfloat16)]


def split_product(left, right):
    count = len(left)
    total = None
    for order in range(count - 1, -1, -1):
        for i in range(order + 1):
            term = jnp.dot(left[i], right[order - i], preferred_element_type=jnp.float32)
            total = term if total is None else total + term
    return total


def newton_kernel(iters, scale, a0, a1, b0, b1, p_ref, w_ref, u_ref, n_ref, r_ref, *rest):
    pieces, (gram, cur) = rest[:-2], rest[-2:]
    rows = gram.shape[0]
    step = rows // PACK
    halves = [a0[...] + a1[...], b0[...] + b1[...]]
    bands = [
        halves[0][:, : 4 * step],
        halves[1][:, : 3 * step],
        halves[1][:, 3 * step :],
        halves[0][:, 4 * step :],
    ]
    eye = lax.broadcasted_iota(jnp.int32, (step, step), 0) == lax.broadcasted_iota(
        jnp.int32, (step, step), 1
    )
    diag = sum(jnp.where(eye, band[:, :step], 0.0) for band in bands)
    norm_sq = jnp.sum(jnp.sum(diag, axis=1, keepdims=True), axis=0, keepdims=True)
    factor = 1.0 / (jnp.sqrt(norm_sq) + norm_epsilon)
    square = factor * factor
    for i, band in enumerate(bands):
        scaled = band * square
        gram[i * step : (i + 1) * step, i * step :] = scaled
        for j in range(i + 1, PACK):
            gram[j * step : (j + 1) * step, i * step : (i + 1) * step] = scaled[
                :, (j - i) * step : (j - i + 1) * step
            ].T
    cur[...] = p_ref[...] * factor

    def mixed_of(a, a_parts):
        return second_coeff * a + third_coeff * split_product(a_parts[:2], a_parts[:2])

    def apply(mixed_parts):
        x = cur[...]
        return first_coeff * x + split_product(mixed_parts[:2], parts_of(x, 2))

    def advance(count):
        a = gram[...]
        a_parts = parts_of(a, count)
        mixed_parts = parts_of(mixed_of(a, a_parts if count == 2 else parts_of(a, 2)), count)
        half_way = first_coeff * a + split_product(mixed_parts, a_parts)
        gram[...] = first_coeff * half_way + split_product(parts_of(half_way, count), mixed_parts)
        cur[...] = apply(mixed_parts)

    advance(3)
    if iters > 2:
        lax.fori_loop(1, iters - 1, lambda _, none: (advance(2), none)[1], 0)
    a = gram[...]
    u = apply(parts_of(mixed_of(a, parts_of(a, 2)), 2)) * scale
    w = w_ref[...]
    new = w - learn_rate * (u + weight_decay * w)
    rounded = new.astype(r_ref.dtype)
    r_ref[...] = rounded
    for i, piece in enumerate(pieces):
        piece[...] = rounded[i * piece.shape[0] : (i + 1) * piece.shape[0]]
    u_ref[...] = u
    n_ref[...] = new


def newton(halves, moved, nesterov, master, iters, scale, chunks):
    rows, cols = nesterov.shape
    vmem = pl.BlockSpec(memory_space=pltpu.VMEM)
    f32 = jax.ShapeDtypeStruct((rows, cols), jnp.float32)
    pieces = [jax.ShapeDtypeStruct((rows // chunks, cols), jnp.bfloat16) for _ in range(chunks)]
    return pl.pallas_call(
        functools.partial(newton_kernel, iters, scale),
        out_shape=[f32, f32, jax.ShapeDtypeStruct((rows, cols), jnp.bfloat16)] + pieces,
        in_specs=[vmem] * 6,
        out_specs=[vmem] * (3 + chunks),
        scratch_shapes=[
            pltpu.VMEM((rows, rows), jnp.float32),
            pltpu.VMEM((rows, cols), jnp.float32),
        ],
        cost_estimate=pl.CostEstimate(
            flops=2 * 60 * rows * rows * cols, bytes_accessed=24 * rows * cols, transcendentals=0
        ),
        compiler_params=pltpu.CompilerParams(vmem_limit_bytes=24 << 20),
    )(halves[0], moved[0], halves[1], moved[1], nesterov, master)


def flipped(block, axis, flip):
    return lax.ppermute(block, axis, [(i, i ^ flip) for i in range(lax.axis_size(axis))])


def owner_of(owned_matrix, quads):
    ids = jnp.arange(quads, dtype=jnp.int32)
    return jnp.sum(
        jnp.where(owned_matrix[:, :, None] == ids[None, None, :], ids[None, :, None], 0), axis=1
    ).reshape(-1)


def wanted_slots(rollout_matrix, owned_matrix, share_count):
    quads = owned_matrix.shape[1]
    group = lax.axis_index("grp")
    place = lax.axis_index("dev")
    inverse = owner_of(owned_matrix, quads)
    mats = jnp.arange(inverse.shape[0], dtype=jnp.int32)
    targets = rollout_matrix[0]
    owner = jnp.sum(jnp.where(targets[:, None] == mats[None, :], inverse[None, :], 0), axis=1)
    slot = ((targets // quads) ^ group) * quads + (owner ^ (place // share_count))
    turns = place ^ jnp.arange(share_count, dtype=jnp.int32)
    places = jnp.arange(slot.shape[0], dtype=jnp.int32)
    return jnp.sum(jnp.where(turns[:, None] == places[None, :], slot[None, :], 0), axis=1)


def pick_kernel(chunk, slots, *refs):
    turns = slots.shape[0]
    slabs, outs, done = refs[: -turns - 1], refs[-turns - 1 : -1], refs[-1]
    rows = outs[0].shape[0]
    views = [
        slab if slab.shape[0] == rows else slab.at[pl.ds(chunk * rows, rows)] for slab in slabs
    ]
    for turn in range(turns):
        slot = slots[turn]
        for index, view in enumerate(views):

            @pl.when(slot == index)
            def _(view=view, turn=turn):
                pltpu.make_async_copy(view, outs[turn], done.at[turn]).start()

    for turn in range(turns):
        pltpu.make_async_copy(views[0], outs[turn], done.at[turn]).wait()


def pick(slots, slabs, chunk, rows):
    turns = slots.shape[0]
    cols = slabs[0].shape[1]
    block = jax.ShapeDtypeStruct((rows, cols), slabs[0].dtype)
    return pl.pallas_call(
        functools.partial(pick_kernel, chunk),
        out_shape=[block] * turns,
        in_specs=[pl.BlockSpec(memory_space=pltpu.SMEM)]
        + [pl.BlockSpec(memory_space=pl.ANY)] * len(slabs),
        out_specs=[pl.BlockSpec(memory_space=pltpu.VMEM)] * turns,
        scratch_shapes=[pltpu.SemaphoreType.DMA((turns,))],
        cost_estimate=pl.CostEstimate(
            flops=0, bytes_accessed=4 * turns * rows * cols, transcendentals=0
        ),
        compiler_params=pltpu.CompilerParams(vmem_limit_bytes=8 << 20),
    )(slots, *slabs)


def lay_kernel(share_count, chunk, *refs):
    mine = lax.axis_index("dev") % share_count
    blocks, out, done = refs[:share_count], refs[-2], refs[-1]
    rows, cols = blocks[0].shape
    moves = []
    for turn, block in enumerate(blocks):
        start = pl.multiple_of((mine ^ turn) * cols, cols)
        place = out.at[pl.ds(chunk * rows, rows), pl.ds(start, cols)]
        moves.append(pltpu.make_async_copy(block, place, done.at[turn]))
    for move in moves:
        move.start()
    for move in moves:
        move.wait()


def lay(blocks, chunk, chunks, before):
    share_count = len(blocks)
    rows, cols = blocks[0].shape
    extra = [] if before is None else [before]
    return pl.pallas_call(
        functools.partial(lay_kernel, share_count, chunk),
        out_shape=jax.ShapeDtypeStruct((rows * chunks, cols * share_count), blocks[0].dtype),
        in_specs=[pl.BlockSpec(memory_space=pltpu.VMEM)] * share_count
        + [pl.BlockSpec(memory_space=pltpu.HBM)] * len(extra),
        out_specs=pl.BlockSpec(memory_space=pltpu.HBM),
        scratch_shapes=[pltpu.SemaphoreType.DMA((share_count,))],
        input_output_aliases={share_count: 0} if extra else {},
        cost_estimate=pl.CostEstimate(
            flops=0, bytes_accessed=4 * share_count * rows * cols, transcendentals=0
        ),
        compiler_params=pltpu.CompilerParams(vmem_limit_bytes=8 << 20),
    )(*blocks, *extra)


def spread(block):
    group_count = lax.axis_size("grp")
    table = {0: block}
    for bit in range(group_count.bit_length() - 2, -1, -1):
        for key in list(table):
            table[key | 1 << bit] = flipped(table[key], "grp", 1 << bit)
    return [table[key] for key in range(group_count)]


def sync_two_halves(rounded, pieces, slots, share_count):
    chunks = len(pieces)
    rows = pieces[0].shape[0]
    others = []
    for piece in pieces:
        others.append(flipped(piece, "dev", share_count))
    mine = spread(rounded)
    result = None
    for chunk in range(chunks):
        theirs = spread(others[chunk])
        slabs = [slab for pair in zip(mine, theirs) for slab in pair]
        blocks = list(pick(slots, slabs, chunk, rows))
        for turn in range(1, share_count):
            blocks[turn] = flipped(blocks[turn], "dev", turn)
        result = lay(blocks, chunk, chunks, result)
    return result


def sync_any(rounded, rollout_matrix, owned_matrix, row_block, columns):
    dev_count = lax.axis_size("dev")
    group_count = lax.axis_size("grp")
    quads = owned_matrix.shape[1]
    row_count, slab_cols = rounded.shape
    all_mats = group_count * quads
    slot_count = all_mats // dev_count
    own_rows = lax.all_to_all(
        rounded.reshape(dev_count, row_block, slab_cols),
        "dev",
        split_axis=0,
        concat_axis=2,
        tiled=True,
    )
    copies = lax.all_gather(own_rows, "grp", axis=0, tiled=True)
    blocks = copies.reshape(group_count, row_block, quads, columns)
    inverse_flat = owner_of(owned_matrix, quads)
    targets = rollout_matrix[0]
    global_ids = jnp.arange(all_mats, dtype=jnp.int32)
    target_group = targets // quads
    target_owner = jnp.sum(
        jnp.where(targets[:, None] == global_ids[None, :], inverse_flat[None, :], 0), axis=1
    )
    flat_owner = target_group * quads + target_owner
    chooser = (
        (flat_owner[:, None] == global_ids[None, :])
        .astype(jnp.bfloat16)
        .reshape(all_mats, group_count, quads)
    )
    outgoing = jnp.einsum(
        "pgq,grqc->prc", chooser, blocks, preferred_element_type=jnp.float32
    ).astype(jnp.bfloat16)
    landed = lax.all_to_all(
        outgoing.reshape(dev_count, slot_count, row_block, columns),
        "dev",
        split_axis=0,
        concat_axis=2,
        tiled=True,
    )
    return landed.reshape(slot_count, row_count, columns)


def step(gradient, momentum, master_weight, owned_matrix, rollout_matrix):
    group = lax.axis_index("grp")
    dev_count = lax.axis_size("dev")
    group_count = lax.axis_size("grp")
    quads = gradient.shape[0]
    row_block = gradient.shape[1]
    columns = gradient.shape[2]
    slab_cols = momentum.shape[2]
    row_count = momentum.shape[1]
    share_count = columns // slab_cols
    two_halves = (
        quads == 2
        and dev_count == quads * share_count
        and not share_count & (share_count - 1)
        and not group_count & (group_count - 1)
    )
    mine = lax.dynamic_index_in_dim(owned_matrix, group, 0, keepdims=False)
    local_ids = jnp.arange(quads, dtype=jnp.int32)
    picker = (mine[:, None] == local_ids[None, :]).astype(jnp.bfloat16)
    ordered = jnp.einsum(
        "qm,mrc->rqc", picker, gradient, preferred_element_type=jnp.float32
    ).astype(jnp.bfloat16)
    arrived = lax.all_to_all(
        ordered.reshape(row_block, dev_count, slab_cols),
        "dev",
        split_axis=1,
        concat_axis=0,
        tiled=True,
    )
    grad_slab = arrived.reshape(row_count, slab_cols).astype(jnp.float32)
    new_moment = momentum_decay * momentum[0] + grad_slab
    nesterov = grad_slab + momentum_decay * new_moment
    if two_halves:
        slots = wanted_slots(rollout_matrix, owned_matrix, share_count)
        nesterov, slots = lax.optimization_barrier((nesterov, slots))
    halves, moved = gram_sum(nesterov, share_count)
    scale_factor = 0.2 * math.sqrt(max(row_count, columns))
    update, new_weight, rounded, *pieces = newton(
        halves, moved, nesterov, master_weight[0], ITERS, scale_factor, CHUNKS if two_halves else 0
    )
    if two_halves:
        rollout = sync_two_halves(rounded, pieces, slots, share_count)[None]
    else:
        rollout = sync_any(rounded, rollout_matrix, owned_matrix, row_block, columns)
    return (new_moment[None], update[None], new_weight[None], rollout)


def solution(mesh):
    placed = (
        P("grp", "dev", None),
        P(("grp", "dev"), None, None),
        P(("grp", "dev"), None, None),
        P(),
        P("grp", None),
    )
    return jax.shard_map(
        step,
        mesh=mesh,
        in_specs=placed,
        out_specs=(
            P(("grp", "dev"), None, None),
            P(("grp", "dev"), None, None),
            P(("grp", "dev"), None, None),
            P(("grp", "dev"), None, None),
        ),
        check_vma=False,
    )
```

```python
import functools
import math

import jax
import jax.numpy as jnp
from jax import lax
from jax.experimental import pallas as pl
from jax.experimental.pallas import tpu as pltpu
from jax.sharding import PartitionSpec as P


ITERS = 5
PACK = 4
CHUNKS = 2


momentum_decay = 0.95
learn_rate = 0.02
weight_decay = 0.1
first_coeff = 3.4445
second_coeff = -4.775
third_coeff = 2.0315
norm_epsilon = 1e-07


def from_partner(block, axis, bit):
    count = lax.axis_size(axis)
    route = []
    for low in range(count):
        high = low | 1 << bit
        if high != low and high < count:
            route += [(low, high), (high, low)]
    return lax.ppermute(block, axis, route)


def parts_of(value, count):
    parts = []
    for _ in range(count - 1):
        high = value.astype(jnp.bfloat16)
        parts.append(high)
        value = value - high.astype(jnp.float32)
    return parts + [value.astype(jnp.bfloat16)]


def split_product(left, right, turned=False):
    count = len(left)
    total = None
    for order in range(count - 1, -1, -1):
        for i in range(order + 1):
            term = lax.dot_general(
                left[i],
                right[order - i],
                (((1,), (1 if turned else 0,)), ((), ())),
                preferred_element_type=jnp.float32,
            )
            total = term if total is None else total + term
    return total


def deal_kernel(share_count, owned, gradient, *refs):
    outs, done = refs[:-1], refs[-1]
    group = lax.axis_index("grp")
    place = lax.axis_index("dev")
    cols = outs[0].shape[1]
    moves = []
    for turn, out in enumerate(outs):
        target = place ^ turn
        column = pl.multiple_of((target % share_count) * cols, cols)
        block = gradient.at[owned[group, target // share_count], :, pl.ds(column, cols)]
        moves.append(pltpu.make_async_copy(block, out, done.at[turn]))
    for move in moves:
        move.start()
    for move in moves:
        move.wait()


def deal(gradient, owned_matrix, share_count):
    quads, rows, columns = gradient.shape
    turns = quads * share_count
    block = jax.ShapeDtypeStruct((rows, columns // share_count), gradient.dtype)
    return pl.pallas_call(
        functools.partial(deal_kernel, share_count),
        out_shape=[block] * turns,
        in_specs=[pl.BlockSpec(memory_space=pltpu.SMEM), pl.BlockSpec(memory_space=pl.ANY)],
        out_specs=[pl.BlockSpec(memory_space=pltpu.VMEM)] * turns,
        scratch_shapes=[pltpu.SemaphoreType.DMA((turns,))],
        cost_estimate=pl.CostEstimate(
            flops=0, bytes_accessed=4 * gradient.size, transcendentals=0
        ),
        compiler_params=pltpu.CompilerParams(vmem_limit_bytes=8 << 20),
    )(owned_matrix, gradient)


def gram_kernel(m_ref, *refs):
    blocks, (nm_ref, p_ref, a_ref, b_ref) = refs[:-4], refs[-4:]
    place = lax.axis_index("dev") if len(blocks) > 1 else 0
    for turn, block in enumerate(blocks):
        size = block.shape[0]
        rows = pl.ds(pl.multiple_of((place ^ turn) * size, size), size)
        grad = block[...].astype(jnp.float32)
        moment = momentum_decay * m_ref[rows, :] + grad
        nm_ref[rows, :] = moment
        p_ref[rows, :] = grad + momentum_decay * moment
    parts = parts_of(p_ref[...], 3)
    step = p_ref.shape[0] // PACK

    def band(i):
        low = i * step
        return split_product(
            [part[low : low + step] for part in parts], [part[low:] for part in parts], turned=True
        )

    for ref, first, second in ((a_ref, 0, 3), (b_ref, 1, 2)):
        width = (PACK - first) * step
        ref[:, :width] = band(first)
        ref[:, width:] = band(second)


def gram_halves(momentum, blocks):
    rows, cols = momentum.shape
    vmem = pl.BlockSpec(memory_space=pltpu.VMEM)
    f32 = jax.ShapeDtypeStruct((rows, cols), jnp.float32)
    half = jax.ShapeDtypeStruct((rows // PACK, rows // PACK * (PACK + 1)), jnp.float32)
    return pl.pallas_call(
        gram_kernel,
        out_shape=[f32, f32, half, half],
        in_specs=[vmem] * (1 + len(blocks)),
        out_specs=[vmem] * 4,
        cost_estimate=pl.CostEstimate(
            flops=8 * rows * rows * cols, bytes_accessed=16 * rows * cols, transcendentals=0
        ),
        compiler_params=pltpu.CompilerParams(vmem_limit_bytes=24 << 20),
    )(momentum, *blocks)


def gram_sum(halves, share_count):
    moved = [jnp.zeros_like(half) for half in halves]
    bits = list(range(share_count.bit_length() - 1))
    orders = [bits, bits[::-1]]
    for turn in range(len(bits)):
        halves = [half + other for half, other in zip(halves, moved)] if turn else halves
        moved = [from_partner(half, "dev", order[turn]) for half, order in zip(halves, orders)]
    return halves, moved


def newton_kernel(iters, scale, a0, a1, b0, b1, p_ref, w_ref, u_ref, n_ref, r_ref, *rest):
    pieces, (gram, cur) = rest[:-2], rest[-2:]
    rows = gram.shape[0]
    step = rows // PACK
    halves = [a0[...] + a1[...], b0[...] + b1[...]]
    bands = [
        halves[0][:, : 4 * step],
        halves[1][:, : 3 * step],
        halves[1][:, 3 * step :],
        halves[0][:, 4 * step :],
    ]
    eye = lax.broadcasted_iota(jnp.int32, (step, step), 0) == lax.broadcasted_iota(
        jnp.int32, (step, step), 1
    )
    diag = sum(jnp.where(eye, band[:, :step], 0.0) for band in bands)
    norm_sq = jnp.sum(jnp.sum(diag, axis=1, keepdims=True), axis=0, keepdims=True)
    factor = 1.0 / (jnp.sqrt(norm_sq) + norm_epsilon)
    square = factor * factor
    for i, band in enumerate(bands):
        scaled = band * square
        gram[i * step : (i + 1) * step, i * step :] = scaled
        for j in range(i + 1, PACK):
            gram[j * step : (j + 1) * step, i * step : (i + 1) * step] = scaled[
                :, (j - i) * step : (j - i + 1) * step
            ].T
    cur[...] = p_ref[...] * factor

    def mixed_of(a, a_parts):
        return second_coeff * a + third_coeff * split_product(a_parts[:2], a_parts[:2])

    def apply(mixed_parts):
        x = cur[...]
        return first_coeff * x + split_product(mixed_parts[:2], parts_of(x, 2))

    def advance(count):
        a = gram[...]
        a_parts = parts_of(a, count)
        mixed_parts = parts_of(mixed_of(a, a_parts if count == 2 else parts_of(a, 2)), count)
        half_way = first_coeff * a + split_product(mixed_parts, a_parts)
        gram[...] = first_coeff * half_way + split_product(parts_of(half_way, count), mixed_parts)
        cur[...] = apply(mixed_parts)

    advance(3)
    if iters > 2:
        lax.fori_loop(1, iters - 1, lambda _, none: (advance(2), none)[1], 0)
    a = gram[...]
    u = apply(parts_of(mixed_of(a, parts_of(a, 2)), 2)) * scale
    w = w_ref[...]
    new = w - learn_rate * (u + weight_decay * w)
    rounded = new.astype(r_ref.dtype)
    r_ref[...] = rounded
    for i, piece in enumerate(pieces):
        piece[...] = rounded[i * piece.shape[0] : (i + 1) * piece.shape[0]]
    u_ref[...] = u
    n_ref[...] = new


def newton(halves, moved, nesterov, master, iters, scale, chunks):
    rows, cols = nesterov.shape
    vmem = pl.BlockSpec(memory_space=pltpu.VMEM)
    f32 = jax.ShapeDtypeStruct((rows, cols), jnp.float32)
    pieces = [jax.ShapeDtypeStruct((rows // chunks, cols), jnp.bfloat16) for _ in range(chunks)]
    return pl.pallas_call(
        functools.partial(newton_kernel, iters, scale),
        out_shape=[f32, f32, jax.ShapeDtypeStruct((rows, cols), jnp.bfloat16)] + pieces,
        in_specs=[vmem] * 6,
        out_specs=[vmem] * (3 + chunks),
        scratch_shapes=[
            pltpu.VMEM((rows, rows), jnp.float32),
            pltpu.VMEM((rows, cols), jnp.float32),
        ],
        cost_estimate=pl.CostEstimate(
            flops=2 * 60 * rows * rows * cols, bytes_accessed=24 * rows * cols, transcendentals=0
        ),
        compiler_params=pltpu.CompilerParams(vmem_limit_bytes=24 << 20),
    )(halves[0], moved[0], halves[1], moved[1], nesterov, master)


def flipped(block, axis, flip):
    return lax.ppermute(block, axis, [(i, i ^ flip) for i in range(lax.axis_size(axis))])


def owner_of(owned_matrix, quads):
    ids = jnp.arange(quads, dtype=jnp.int32)
    return jnp.sum(
        jnp.where(owned_matrix[:, :, None] == ids[None, None, :], ids[None, :, None], 0), axis=1
    ).reshape(-1)


def wanted_slots(rollout_matrix, owned_matrix, share_count):
    quads = owned_matrix.shape[1]
    group = lax.axis_index("grp")
    place = lax.axis_index("dev")
    inverse = owner_of(owned_matrix, quads)
    mats = jnp.arange(inverse.shape[0], dtype=jnp.int32)
    targets = rollout_matrix[0]
    owner = jnp.sum(jnp.where(targets[:, None] == mats[None, :], inverse[None, :], 0), axis=1)
    slot = ((targets // quads) ^ group) * quads + (owner ^ (place // share_count))
    turns = place ^ jnp.arange(share_count, dtype=jnp.int32)
    places = jnp.arange(slot.shape[0], dtype=jnp.int32)
    return jnp.sum(jnp.where(turns[:, None] == places[None, :], slot[None, :], 0), axis=1)


def pick_kernel(chunk, slots, *refs):
    turns = slots.shape[0]
    slabs, outs, done = refs[: -turns - 1], refs[-turns - 1 : -1], refs[-1]
    rows = outs[0].shape[0]
    views = [
        slab if slab.shape[0] == rows else slab.at[pl.ds(chunk * rows, rows)] for slab in slabs
    ]
    for turn in range(turns):
        slot = slots[turn]
        for index, view in enumerate(views):

            @pl.when(slot == index)
            def _(view=view, turn=turn):
                pltpu.make_async_copy(view, outs[turn], done.at[turn]).start()

    for turn in range(turns):
        pltpu.make_async_copy(views[0], outs[turn], done.at[turn]).wait()


def pick(slots, slabs, chunk, rows):
    turns = slots.shape[0]
    cols = slabs[0].shape[1]
    block = jax.ShapeDtypeStruct((rows, cols), slabs[0].dtype)
    return pl.pallas_call(
        functools.partial(pick_kernel, chunk),
        out_shape=[block] * turns,
        in_specs=[pl.BlockSpec(memory_space=pltpu.SMEM)]
        + [pl.BlockSpec(memory_space=pl.ANY)] * len(slabs),
        out_specs=[pl.BlockSpec(memory_space=pltpu.VMEM)] * turns,
        scratch_shapes=[pltpu.SemaphoreType.DMA((turns,))],
        cost_estimate=pl.CostEstimate(
            flops=0, bytes_accessed=4 * turns * rows * cols, transcendentals=0
        ),
        compiler_params=pltpu.CompilerParams(vmem_limit_bytes=8 << 20),
    )(slots, *slabs)


def lay_kernel(share_count, chunk, *refs):
    mine = lax.axis_index("dev") % share_count
    blocks, out, done = refs[:share_count], refs[-2], refs[-1]
    rows, cols = blocks[0].shape
    moves = []
    for turn, block in enumerate(blocks):
        start = pl.multiple_of((mine ^ turn) * cols, cols)
        place = out.at[pl.ds(chunk * rows, rows), pl.ds(start, cols)]
        moves.append(pltpu.make_async_copy(block, place, done.at[turn]))
    for move in moves:
        move.start()
    for move in moves:
        move.wait()


def lay(blocks, chunk, chunks, before):
    share_count = len(blocks)
    rows, cols = blocks[0].shape
    extra = [] if before is None else [before]
    return pl.pallas_call(
        functools.partial(lay_kernel, share_count, chunk),
        out_shape=jax.ShapeDtypeStruct((rows * chunks, cols * share_count), blocks[0].dtype),
        in_specs=[pl.BlockSpec(memory_space=pltpu.VMEM)] * share_count
        + [pl.BlockSpec(memory_space=pltpu.HBM)] * len(extra),
        out_specs=pl.BlockSpec(memory_space=pltpu.HBM),
        scratch_shapes=[pltpu.SemaphoreType.DMA((share_count,))],
        input_output_aliases={share_count: 0} if extra else {},
        cost_estimate=pl.CostEstimate(
            flops=0, bytes_accessed=4 * share_count * rows * cols, transcendentals=0
        ),
        compiler_params=pltpu.CompilerParams(vmem_limit_bytes=8 << 20),
    )(*blocks, *extra)


def spread(block):
    group_count = lax.axis_size("grp")
    table = {0: block}
    for bit in range(group_count.bit_length() - 2, -1, -1):
        for key in list(table):
            table[key | 1 << bit] = flipped(table[key], "grp", 1 << bit)
    return [table[key] for key in range(group_count)]


def sync_two_halves(rounded, pieces, slots, share_count):
    chunks = len(pieces)
    rows = pieces[0].shape[0]
    others = []
    for piece in pieces:
        others.append(flipped(piece, "dev", share_count))
    mine = spread(rounded)
    result = None
    for chunk in range(chunks):
        theirs = spread(others[chunk])
        slabs = [slab for pair in zip(mine, theirs) for slab in pair]
        blocks = list(pick(slots, slabs, chunk, rows))
        for turn in range(1, share_count):
            blocks[turn] = flipped(blocks[turn], "dev", turn)
        result = lay(blocks, chunk, chunks, result)
    return result


def sync_any(rounded, rollout_matrix, owned_matrix, row_block, columns):
    dev_count = lax.axis_size("dev")
    group_count = lax.axis_size("grp")
    quads = owned_matrix.shape[1]
    row_count, slab_cols = rounded.shape
    all_mats = group_count * quads
    slot_count = all_mats // dev_count
    own_rows = lax.all_to_all(
        rounded.reshape(dev_count, row_block, slab_cols),
        "dev",
        split_axis=0,
        concat_axis=2,
        tiled=True,
    )
    copies = lax.all_gather(own_rows, "grp", axis=0, tiled=True)
    blocks = copies.reshape(group_count, row_block, quads, columns)
    inverse_flat = owner_of(owned_matrix, quads)
    targets = rollout_matrix[0]
    global_ids = jnp.arange(all_mats, dtype=jnp.int32)
    target_group = targets // quads
    target_owner = jnp.sum(
        jnp.where(targets[:, None] == global_ids[None, :], inverse_flat[None, :], 0), axis=1
    )
    flat_owner = target_group * quads + target_owner
    chooser = (
        (flat_owner[:, None] == global_ids[None, :])
        .astype(jnp.bfloat16)
        .reshape(all_mats, group_count, quads)
    )
    outgoing = jnp.einsum(
        "pgq,grqc->prc", chooser, blocks, preferred_element_type=jnp.float32
    ).astype(jnp.bfloat16)
    landed = lax.all_to_all(
        outgoing.reshape(dev_count, slot_count, row_block, columns),
        "dev",
        split_axis=0,
        concat_axis=2,
        tiled=True,
    )
    return landed.reshape(slot_count, row_count, columns)


def step(gradient, momentum, master_weight, owned_matrix, rollout_matrix):
    group = lax.axis_index("grp")
    dev_count = lax.axis_size("dev")
    group_count = lax.axis_size("grp")
    quads = gradient.shape[0]
    row_block = gradient.shape[1]
    columns = gradient.shape[2]
    slab_cols = momentum.shape[2]
    row_count = momentum.shape[1]
    share_count = columns // slab_cols
    two_halves = (
        quads == 2
        and dev_count == quads * share_count
        and not share_count & (share_count - 1)
        and not group_count & (group_count - 1)
    )
    two_halves = (
        quads == 2
        and dev_count == quads * share_count
        and not share_count & (share_count - 1)
        and not group_count & (group_count - 1)
    )
    if two_halves:
        dealt = list(deal(gradient, owned_matrix, share_count))
        for turn in [*range(share_count, dev_count), *range(1, share_count)]:
            dealt[turn] = flipped(dealt[turn], "dev", turn)
        slots = wanted_slots(rollout_matrix, owned_matrix, share_count)
    else:
        mine = lax.dynamic_index_in_dim(owned_matrix, group, 0, keepdims=False)
        local_ids = jnp.arange(quads, dtype=jnp.int32)
        picker = (mine[:, None] == local_ids[None, :]).astype(jnp.bfloat16)
        ordered = jnp.einsum(
            "qm,mrc->rqc", picker, gradient, preferred_element_type=jnp.float32
        ).astype(jnp.bfloat16)
        arrived = lax.all_to_all(
            ordered.reshape(row_block, dev_count, slab_cols),
            "dev",
            split_axis=1,
            concat_axis=0,
            tiled=True,
        )
        dealt = [arrived.reshape(row_count, slab_cols)]
    new_moment, nesterov, *halves = gram_halves(momentum[0], dealt)
    if two_halves:
        halves, slots = lax.optimization_barrier((halves, slots))
    halves, moved = gram_sum(halves, share_count)
    scale_factor = 0.2 * math.sqrt(max(row_count, columns))
    update, new_weight, rounded, *pieces = newton(
        halves, moved, nesterov, master_weight[0], ITERS, scale_factor, CHUNKS if two_halves else 0
    )
    if two_halves:
        rollout = sync_two_halves(rounded, pieces, slots, share_count)[None]
    else:
        rollout = sync_any(rounded, rollout_matrix, owned_matrix, row_block, columns)
    return (new_moment[None], update[None], new_weight[None], rollout)


def solution(mesh):
    placed = (
        P("grp", "dev", None),
        P(("grp", "dev"), None, None),
        P(("grp", "dev"), None, None),
        P(),
        P("grp", None),
    )
    return jax.shard_map(
        step,
        mesh=mesh,
        in_specs=placed,
        out_specs=(
            P(("grp", "dev"), None, None),
            P(("grp", "dev"), None, None),
            P(("grp", "dev"), None, None),
            P(("grp", "dev"), None, None),
        ),
        check_vma=False,
    )
```

```python
import functools
import math

import jax
import jax.numpy as jnp
from jax import lax
from jax.experimental import pallas as pl
from jax.experimental.pallas import tpu as pltpu
from jax.sharding import PartitionSpec as P


ITERS = 5
PACK = 4
STRIP = 8
CHUNKS = 2


momentum_decay = 0.95
learn_rate = 0.02
weight_decay = 0.1
first_coeff = 3.4445
second_coeff = -4.775
third_coeff = 2.0315
norm_epsilon = 1e-07


def from_partner(block, axis, bit):
    count = lax.axis_size(axis)
    route = []
    for low in range(count):
        high = low | 1 << bit
        if high != low and high < count:
            route += [(low, high), (high, low)]
    return lax.ppermute(block, axis, route)


def parts_of(value, count):
    parts = []
    for _ in range(count - 1):
        high = value.astype(jnp.bfloat16)
        parts.append(high)
        value = value - high.astype(jnp.float32)
    return parts + [value.astype(jnp.bfloat16)]


def square_indices(size):
    return [lax.broadcasted_iota(jnp.int32, (size, size), axis) for axis in range(2)]


def split_product(left, right, turned=False):
    count = len(left)
    total = None
    for order in range(count - 1, -1, -1):
        for i in range(order + 1):
            term = lax.dot_general(
                left[i],
                right[order - i],
                (((1,), (1 if turned else 0,)), ((), ())),
                preferred_element_type=jnp.float32,
            )
            total = term if total is None else total + term
    return total


def even_product(left, right):
    half = left[0].shape[0] // 2
    top = split_product([part[:half] for part in left], right)
    low = split_product([part[half:] for part in left], [part[:, half:] for part in right])
    bottom = jnp.concatenate([top[:, half:].T, low], axis=1)
    return jnp.concatenate([top, bottom], axis=0)


def deal_kernel(share_count, owned, gradient, *refs):
    outs, done = refs[:-1], refs[-1]
    group = lax.axis_index("grp")
    place = lax.axis_index("dev")
    cols = outs[0].shape[1]
    moves = []
    for turn, out in enumerate(outs):
        target = place ^ turn
        column = pl.multiple_of((target % share_count) * cols, cols)
        block = gradient.at[owned[group, target // share_count], :, pl.ds(column, cols)]
        moves.append(pltpu.make_async_copy(block, out, done.at[turn]))
    for move in moves:
        move.start()
    for move in moves:
        move.wait()


def deal(gradient, owned_matrix, share_count):
    quads, rows, columns = gradient.shape
    turns = quads * share_count
    block = jax.ShapeDtypeStruct((rows, columns // share_count), gradient.dtype)
    return pl.pallas_call(
        functools.partial(deal_kernel, share_count),
        out_shape=[block] * turns,
        in_specs=[pl.BlockSpec(memory_space=pltpu.SMEM), pl.BlockSpec(memory_space=pl.ANY)],
        out_specs=[pl.BlockSpec(memory_space=pltpu.VMEM)] * turns,
        scratch_shapes=[pltpu.SemaphoreType.DMA((turns,))],
        cost_estimate=pl.CostEstimate(
            flops=0, bytes_accessed=4 * gradient.size, transcendentals=0
        ),
        compiler_params=pltpu.CompilerParams(vmem_limit_bytes=8 << 20),
    )(owned_matrix, gradient)


def gram_kernel(m_ref, *refs):
    blocks, (nm_ref, p_ref, a_ref, b_ref) = refs[:-4], refs[-4:]
    place = lax.axis_index("dev") if len(blocks) > 1 else 0
    for turn, block in enumerate(blocks):
        size = block.shape[0]
        rows = pl.ds(pl.multiple_of((place ^ turn) * size, size), size)
        grad = block[...].astype(jnp.float32)
        moment = momentum_decay * m_ref[rows, :] + grad
        nm_ref[rows, :] = moment
        p_ref[rows, :] = grad + momentum_decay * moment
    parts = parts_of(p_ref[...], 3)
    step = p_ref.shape[0] // PACK
    row, col = square_indices(step)

    def band(i):
        low = i * step
        return split_product(
            [part[low : low + step] for part in parts], [part[low:] for part in parts], turned=True
        )

    for ref, first, second in ((a_ref, 0, 3), (b_ref, 1, 2)):
        one, two = band(first), band(second)
        ref[:step, :step] = jnp.where(row <= col, one[:, :step], two[:, :step])
        middle = (PACK - first) * step
        ref[:step, step:middle] = one[:, step:]
        if second < PACK - 1:
            ref[:step, middle:] = two[:, step:]
        ref[step:, :] = jnp.zeros((STRIP, ref.shape[1]), jnp.float32)
        diagonal = jnp.sum(jnp.where(row == col, two[:, :step], 0.0), axis=0, keepdims=True)
        ref[step:, :step] = jnp.broadcast_to(diagonal, (STRIP, step))


def gram_halves(momentum, blocks):
    rows, cols = momentum.shape
    vmem = pl.BlockSpec(memory_space=pltpu.VMEM)
    f32 = jax.ShapeDtypeStruct((rows, cols), jnp.float32)
    half = jax.ShapeDtypeStruct((rows // PACK + STRIP, rows), jnp.float32)
    return pl.pallas_call(
        gram_kernel,
        out_shape=[f32, f32, half, half],
        in_specs=[vmem] * (1 + len(blocks)),
        out_specs=[vmem] * 4,
        cost_estimate=pl.CostEstimate(
            flops=8 * rows * rows * cols, bytes_accessed=16 * rows * cols, transcendentals=0
        ),
        compiler_params=pltpu.CompilerParams(vmem_limit_bytes=24 << 20),
    )(momentum, *blocks)


def gram_sum(halves, share_count):
    moved = [jnp.zeros_like(half) for half in halves]
    bits = list(range(share_count.bit_length() - 1))
    orders = [bits, bits[::-1]]
    for turn in range(len(bits)):
        halves = [half + other for half, other in zip(halves, moved)] if turn else halves
        moved = [from_partner(half, "dev", order[turn]) for half, order in zip(halves, orders)]
    return halves, moved


def newton_kernel(iters, scale, a0, a1, b0, b1, p_ref, w_ref, u_ref, n_ref, r_ref, *rest):
    pieces, (gram, cur) = rest[:-2], rest[-2:]
    rows = gram.shape[0]
    step = rows // PACK
    halves = [a0[...] + a1[...], b0[...] + b1[...]]
    row, col = square_indices(step)
    diagonals, norm_sq = [None] * PACK, 0.0
    for half, first, second in zip(halves, (0, 1), (3, 2)):
        block = half[:step, :step]
        upper, lower = jnp.where(row < col, block, 0.0), jnp.where(row > col, block, 0.0)
        one = jnp.where(row == col, block, 0.0)
        two = jnp.where(row == col, half[step : step + 1, :step], 0.0)
        both = jnp.sum(one + two, axis=1, keepdims=True)
        norm_sq = norm_sq + jnp.sum(both, axis=0, keepdims=True)
        diagonals[first] = upper + upper.T + one
        diagonals[second] = lower + lower.T + two
    factor = 1.0 / (jnp.sqrt(norm_sq) + norm_epsilon)
    square = factor * factor
    middle = [(PACK - i) * step for i in range(PACK)]
    bands = [
        halves[0][:step, step : middle[0]],
        halves[1][:step, step : middle[1]],
        halves[1][:step, middle[1] :],
    ]
    for i, diagonal in enumerate(diagonals):
        gram[i * step : (i + 1) * step, i * step : (i + 1) * step] = diagonal * square
    for i, band in enumerate(bands):
        scaled = band * square
        gram[i * step : (i + 1) * step, (i + 1) * step :] = scaled
        for j in range(i + 1, PACK):
            gram[j * step : (j + 1) * step, i * step : (i + 1) * step] = scaled[
                :, (j - i - 1) * step : (j - i) * step
            ].T
    cur[...] = p_ref[...] * factor

    def mixed_of(a, a_parts):
        return second_coeff * a + third_coeff * even_product(a_parts[:2], a_parts[:2])

    def apply(mixed_parts):
        x = cur[...]
        return first_coeff * x + split_product(mixed_parts[:2], parts_of(x, 2))

    def advance(count):
        a = gram[...]
        a_parts = parts_of(a, count)
        mixed_parts = parts_of(mixed_of(a, a_parts if count == 2 else parts_of(a, 2)), count)
        half_way = first_coeff * a + even_product(mixed_parts, a_parts)
        gram[...] = first_coeff * half_way + even_product(
            parts_of(half_way, count), mixed_parts
        )
        cur[...] = apply(mixed_parts)

    advance(3)
    if iters > 2:
        lax.fori_loop(1, iters - 1, lambda _, none: (advance(2), none)[1], 0)
    a = gram[...]
    u = apply(parts_of(mixed_of(a, parts_of(a, 2)), 2)) * scale
    w = w_ref[...]
    new = w - learn_rate * (u + weight_decay * w)
    rounded = new.astype(r_ref.dtype)
    r_ref[...] = rounded
    for i, piece in enumerate(pieces):
        piece[...] = rounded[i * piece.shape[0] : (i + 1) * piece.shape[0]]
    u_ref[...] = u
    n_ref[...] = new


def newton(halves, moved, nesterov, master, iters, scale, chunks):
    rows, cols = nesterov.shape
    vmem = pl.BlockSpec(memory_space=pltpu.VMEM)
    f32 = jax.ShapeDtypeStruct((rows, cols), jnp.float32)
    pieces = [jax.ShapeDtypeStruct((rows // chunks, cols), jnp.bfloat16) for _ in range(chunks)]
    return pl.pallas_call(
        functools.partial(newton_kernel, iters, scale),
        out_shape=[f32, f32, jax.ShapeDtypeStruct((rows, cols), jnp.bfloat16)] + pieces,
        in_specs=[vmem] * 6,
        out_specs=[vmem] * (3 + chunks),
        scratch_shapes=[
            pltpu.VMEM((rows, rows), jnp.float32),
            pltpu.VMEM((rows, cols), jnp.float32),
        ],
        cost_estimate=pl.CostEstimate(
            flops=2 * 60 * rows * rows * cols, bytes_accessed=24 * rows * cols, transcendentals=0
        ),
        compiler_params=pltpu.CompilerParams(vmem_limit_bytes=24 << 20),
    )(halves[0], moved[0], halves[1], moved[1], nesterov, master)


def flipped(block, axis, flip):
    return lax.ppermute(block, axis, [(i, i ^ flip) for i in range(lax.axis_size(axis))])


def owner_of(owned_matrix, quads):
    ids = jnp.arange(quads, dtype=jnp.int32)
    return jnp.sum(
        jnp.where(owned_matrix[:, :, None] == ids[None, None, :], ids[None, :, None], 0), axis=1
    ).reshape(-1)


def wanted_slots(rollout_matrix, owned_matrix, share_count):
    quads = owned_matrix.shape[1]
    group = lax.axis_index("grp")
    place = lax.axis_index("dev")
    inverse = owner_of(owned_matrix, quads)
    mats = jnp.arange(inverse.shape[0], dtype=jnp.int32)
    targets = rollout_matrix[0]
    owner = jnp.sum(jnp.where(targets[:, None] == mats[None, :], inverse[None, :], 0), axis=1)
    slot = ((targets // quads) ^ group) * quads + (owner ^ (place // share_count))
    turns = place ^ jnp.arange(share_count, dtype=jnp.int32)
    places = jnp.arange(slot.shape[0], dtype=jnp.int32)
    return jnp.sum(jnp.where(turns[:, None] == places[None, :], slot[None, :], 0), axis=1)


def pick_kernel(chunk, slots, *refs):
    turns = slots.shape[0]
    slabs, outs, done = refs[: -turns - 1], refs[-turns - 1 : -1], refs[-1]
    rows = outs[0].shape[0]
    views = [
        slab if slab.shape[0] == rows else slab.at[pl.ds(chunk * rows, rows)] for slab in slabs
    ]
    for turn in range(turns):
        slot = slots[turn]
        for index, view in enumerate(views):

            @pl.when(slot == index)
            def _(view=view, turn=turn):
                pltpu.make_async_copy(view, outs[turn], done.at[turn]).start()

    for turn in range(turns):
        pltpu.make_async_copy(views[0], outs[turn], done.at[turn]).wait()


def pick(slots, slabs, chunk, rows):
    turns = slots.shape[0]
    cols = slabs[0].shape[1]
    block = jax.ShapeDtypeStruct((rows, cols), slabs[0].dtype)
    return pl.pallas_call(
        functools.partial(pick_kernel, chunk),
        out_shape=[block] * turns,
        in_specs=[pl.BlockSpec(memory_space=pltpu.SMEM)]
        + [pl.BlockSpec(memory_space=pl.ANY)] * len(slabs),
        out_specs=[pl.BlockSpec(memory_space=pltpu.VMEM)] * turns,
        scratch_shapes=[pltpu.SemaphoreType.DMA((turns,))],
        cost_estimate=pl.CostEstimate(
            flops=0, bytes_accessed=4 * turns * rows * cols, transcendentals=0
        ),
        compiler_params=pltpu.CompilerParams(vmem_limit_bytes=8 << 20),
    )(slots, *slabs)


def lay_kernel(share_count, chunk, *refs):
    mine = lax.axis_index("dev") % share_count
    blocks, out, done = refs[:share_count], refs[-2], refs[-1]
    rows, cols = blocks[0].shape
    moves = []
    for turn, block in enumerate(blocks):
        start = pl.multiple_of((mine ^ turn) * cols, cols)
        place = out.at[pl.ds(chunk * rows, rows), pl.ds(start, cols)]
        moves.append(pltpu.make_async_copy(block, place, done.at[turn]))
    for move in moves:
        move.start()
    for move in moves:
        move.wait()


def lay(blocks, chunk, chunks, before):
    share_count = len(blocks)
    rows, cols = blocks[0].shape
    extra = [] if before is None else [before]
    return pl.pallas_call(
        functools.partial(lay_kernel, share_count, chunk),
        out_shape=jax.ShapeDtypeStruct((rows * chunks, cols * share_count), blocks[0].dtype),
        in_specs=[pl.BlockSpec(memory_space=pltpu.VMEM)] * share_count
        + [pl.BlockSpec(memory_space=pltpu.HBM)] * len(extra),
        out_specs=pl.BlockSpec(memory_space=pltpu.HBM),
        scratch_shapes=[pltpu.SemaphoreType.DMA((share_count,))],
        input_output_aliases={share_count: 0} if extra else {},
        cost_estimate=pl.CostEstimate(
            flops=0, bytes_accessed=4 * share_count * rows * cols, transcendentals=0
        ),
        compiler_params=pltpu.CompilerParams(vmem_limit_bytes=8 << 20),
    )(*blocks, *extra)


def spread(block):
    group_count = lax.axis_size("grp")
    table = {0: block}
    for bit in range(group_count.bit_length() - 2, -1, -1):
        for key in list(table):
            table[key | 1 << bit] = flipped(table[key], "grp", 1 << bit)
    return [table[key] for key in range(group_count)]


def sync_two_halves(rounded, pieces, slots, share_count):
    chunks = len(pieces)
    rows = pieces[0].shape[0]
    others = []
    for piece in pieces:
        others.append(flipped(piece, "dev", share_count))
    mine = spread(rounded)
    result = None
    for chunk in range(chunks):
        theirs = spread(others[chunk])
        slabs = [slab for pair in zip(mine, theirs) for slab in pair]
        blocks = list(pick(slots, slabs, chunk, rows))
        for turn in range(1, share_count):
            blocks[turn] = flipped(blocks[turn], "dev", turn)
        result = lay(blocks, chunk, chunks, result)
    return result


def sync_any(rounded, rollout_matrix, owned_matrix, row_block, columns):
    dev_count = lax.axis_size("dev")
    group_count = lax.axis_size("grp")
    quads = owned_matrix.shape[1]
    row_count, slab_cols = rounded.shape
    all_mats = group_count * quads
    slot_count = all_mats // dev_count
    own_rows = lax.all_to_all(
        rounded.reshape(dev_count, row_block, slab_cols),
        "dev",
        split_axis=0,
        concat_axis=2,
        tiled=True,
    )
    copies = lax.all_gather(own_rows, "grp", axis=0, tiled=True)
    blocks = copies.reshape(group_count, row_block, quads, columns)
    inverse_flat = owner_of(owned_matrix, quads)
    targets = rollout_matrix[0]
    global_ids = jnp.arange(all_mats, dtype=jnp.int32)
    target_group = targets // quads
    target_owner = jnp.sum(
        jnp.where(targets[:, None] == global_ids[None, :], inverse_flat[None, :], 0), axis=1
    )
    flat_owner = target_group * quads + target_owner
    chooser = (
        (flat_owner[:, None] == global_ids[None, :])
        .astype(jnp.bfloat16)
        .reshape(all_mats, group_count, quads)
    )
    outgoing = jnp.einsum(
        "pgq,grqc->prc", chooser, blocks, preferred_element_type=jnp.float32
    ).astype(jnp.bfloat16)
    landed = lax.all_to_all(
        outgoing.reshape(dev_count, slot_count, row_block, columns),
        "dev",
        split_axis=0,
        concat_axis=2,
        tiled=True,
    )
    return landed.reshape(slot_count, row_count, columns)


def step(gradient, momentum, master_weight, owned_matrix, rollout_matrix):
    group = lax.axis_index("grp")
    dev_count = lax.axis_size("dev")
    group_count = lax.axis_size("grp")
    quads = gradient.shape[0]
    row_block = gradient.shape[1]
    columns = gradient.shape[2]
    slab_cols = momentum.shape[2]
    row_count = momentum.shape[1]
    share_count = columns // slab_cols
    two_halves = (
        quads == 2
        and dev_count == quads * share_count
        and not share_count & (share_count - 1)
        and not group_count & (group_count - 1)
    )
    two_halves = (
        quads == 2
        and dev_count == quads * share_count
        and not share_count & (share_count - 1)
        and not group_count & (group_count - 1)
    )
    if two_halves:
        dealt = list(deal(gradient, owned_matrix, share_count))
        for turn in [*range(share_count, dev_count), *range(1, share_count)]:
            dealt[turn] = flipped(dealt[turn], "dev", turn)
        slots = wanted_slots(rollout_matrix, owned_matrix, share_count)
    else:
        mine = lax.dynamic_index_in_dim(owned_matrix, group, 0, keepdims=False)
        local_ids = jnp.arange(quads, dtype=jnp.int32)
        picker = (mine[:, None] == local_ids[None, :]).astype(jnp.bfloat16)
        ordered = jnp.einsum(
            "qm,mrc->rqc", picker, gradient, preferred_element_type=jnp.float32
        ).astype(jnp.bfloat16)
        arrived = lax.all_to_all(
            ordered.reshape(row_block, dev_count, slab_cols),
            "dev",
            split_axis=1,
            concat_axis=0,
            tiled=True,
        )
        dealt = [arrived.reshape(row_count, slab_cols)]
    new_moment, nesterov, *halves = gram_halves(momentum[0], dealt)
    if two_halves:
        halves, slots = lax.optimization_barrier((halves, slots))
    halves, moved = gram_sum(halves, share_count)
    scale_factor = 0.2 * math.sqrt(max(row_count, columns))
    update, new_weight, rounded, *pieces = newton(
        halves, moved, nesterov, master_weight[0], ITERS, scale_factor, CHUNKS if two_halves else 0
    )
    if two_halves:
        rollout = sync_two_halves(rounded, pieces, slots, share_count)[None]
    else:
        rollout = sync_any(rounded, rollout_matrix, owned_matrix, row_block, columns)
    return (new_moment[None], update[None], new_weight[None], rollout)


def solution(mesh):
    placed = (
        P("grp", "dev", None),
        P(("grp", "dev"), None, None),
        P(("grp", "dev"), None, None),
        P(),
        P("grp", None),
    )
    return jax.shard_map(
        step,
        mesh=mesh,
        in_specs=placed,
        out_specs=(
            P(("grp", "dev"), None, None),
            P(("grp", "dev"), None, None),
            P(("grp", "dev"), None, None),
            P(("grp", "dev"), None, None),
        ),
        check_vma=False,
    )
```

```python
import functools
import math

import jax
import jax.numpy as jnp
from jax import lax
from jax.experimental import pallas as pl
from jax.experimental.pallas import tpu as pltpu
from jax.sharding import PartitionSpec as P


ITERS = 5
PACK = 4
STRIP = 8
CHUNKS = 2


momentum_decay = 0.95
learn_rate = 0.02
weight_decay = 0.1
first_coeff = 3.4445
second_coeff = -4.775
third_coeff = 2.0315
norm_epsilon = 1e-07


def from_partner(block, axis, bit):
    count = lax.axis_size(axis)
    route = []
    for low in range(count):
        high = low | 1 << bit
        if high != low and high < count:
            route += [(low, high), (high, low)]
    return lax.ppermute(block, axis, route)


def parts_of(value, count):
    parts = []
    for _ in range(count - 1):
        high = value.astype(jnp.bfloat16)
        parts.append(high)
        value = value - high.astype(jnp.float32)
    return parts + [value.astype(jnp.bfloat16)]


def square_indices(size):
    return [lax.broadcasted_iota(jnp.int32, (size, size), axis) for axis in range(2)]


def split_product(left, right, turned=False):
    count = len(left)
    terms = [(i, order - i) for order in range(count - 1, -1, -1) for i in range(order + 1)]
    axis = 1 if turned else 0
    return lax.dot_general(
        jnp.concatenate([left[i] for i, _ in terms], axis=1),
        jnp.concatenate([right[j] for _, j in terms], axis=axis),
        (((1,), (axis,)), ((), ())),
        preferred_element_type=jnp.float32,
    )


def even_product(left, right):
    half = left[0].shape[0] // 2
    top = split_product([part[:half] for part in left], right)
    low = split_product([part[half:] for part in left], [part[:, half:] for part in right])
    bottom = jnp.concatenate([top[:, half:].T, low], axis=1)
    return jnp.concatenate([top, bottom], axis=0)


def deal_kernel(share_count, owned, gradient, *refs):
    outs, done = refs[:-1], refs[-1]
    group = lax.axis_index("grp")
    place = lax.axis_index("dev")
    cols = outs[0].shape[1]
    moves = []
    for turn, out in enumerate(outs):
        target = place ^ turn
        column = pl.multiple_of((target % share_count) * cols, cols)
        block = gradient.at[owned[group, target // share_count], :, pl.ds(column, cols)]
        moves.append(pltpu.make_async_copy(block, out, done.at[turn]))
    for move in moves:
        move.start()
    for move in moves:
        move.wait()


def deal(gradient, owned_matrix, share_count):
    quads, rows, columns = gradient.shape
    turns = quads * share_count
    block = jax.ShapeDtypeStruct((rows, columns // share_count), gradient.dtype)
    return pl.pallas_call(
        functools.partial(deal_kernel, share_count),
        out_shape=[block] * turns,
        in_specs=[pl.BlockSpec(memory_space=pltpu.SMEM), pl.BlockSpec(memory_space=pl.ANY)],
        out_specs=[pl.BlockSpec(memory_space=pltpu.VMEM)] * turns,
        scratch_shapes=[pltpu.SemaphoreType.DMA((turns,))],
        cost_estimate=pl.CostEstimate(
            flops=0, bytes_accessed=4 * gradient.size, transcendentals=0
        ),
        compiler_params=pltpu.CompilerParams(vmem_limit_bytes=8 << 20),
    )(owned_matrix, gradient)


def gram_kernel(m_ref, *refs):
    blocks, (nm_ref, p_ref, a_ref, b_ref) = refs[:-4], refs[-4:]
    place = lax.axis_index("dev") if len(blocks) > 1 else 0
    for turn, block in enumerate(blocks):
        size = block.shape[0]
        rows = pl.ds(pl.multiple_of((place ^ turn) * size, size), size)
        grad = block[...].astype(jnp.float32)
        moment = momentum_decay * m_ref[rows, :] + grad
        nm_ref[rows, :] = moment
        p_ref[rows, :] = grad + momentum_decay * moment
    parts = parts_of(p_ref[...], 3)
    step = p_ref.shape[0] // PACK
    row, col = square_indices(step)

    def band(i):
        low = i * step
        return split_product(
            [part[low : low + step] for part in parts], [part[low:] for part in parts], turned=True
        )

    for ref, first, second in ((a_ref, 0, 3), (b_ref, 1, 2)):
        one, two = band(first), band(second)
        ref[:step, :step] = jnp.where(row <= col, one[:, :step], two[:, :step])
        middle = (PACK - first) * step
        ref[:step, step:middle] = one[:, step:]
        if second < PACK - 1:
            ref[:step, middle:] = two[:, step:]
        ref[step:, :] = jnp.zeros((STRIP, ref.shape[1]), jnp.float32)
        diagonal = jnp.sum(jnp.where(row == col, two[:, :step], 0.0), axis=0, keepdims=True)
        ref[step:, :step] = jnp.broadcast_to(diagonal, (STRIP, step))


def gram_halves(momentum, blocks):
    rows, cols = momentum.shape
    vmem = pl.BlockSpec(memory_space=pltpu.VMEM)
    f32 = jax.ShapeDtypeStruct((rows, cols), jnp.float32)
    half = jax.ShapeDtypeStruct((rows // PACK + STRIP, rows), jnp.float32)
    return pl.pallas_call(
        gram_kernel,
        out_shape=[f32, f32, half, half],
        in_specs=[vmem] * (1 + len(blocks)),
        out_specs=[vmem] * 4,
        cost_estimate=pl.CostEstimate(
            flops=8 * rows * rows * cols, bytes_accessed=16 * rows * cols, transcendentals=0
        ),
        compiler_params=pltpu.CompilerParams(vmem_limit_bytes=24 << 20),
    )(momentum, *blocks)


def gram_sum(halves, share_count):
    moved = [jnp.zeros_like(half) for half in halves]
    bits = list(range(share_count.bit_length() - 1))
    orders = [bits, bits[::-1]]
    for turn in range(len(bits)):
        halves = [half + other for half, other in zip(halves, moved)] if turn else halves
        moved = [from_partner(half, "dev", order[turn]) for half, order in zip(halves, orders)]
    return halves, moved


def newton_kernel(iters, scale, a0, a1, b0, b1, p_ref, w_ref, u_ref, r_ref, *rest):
    pieces, (gram, cur) = rest[:-2], rest[-2:]
    rows = gram.shape[0]
    step = rows // PACK
    halves = [a0[...] + a1[...], b0[...] + b1[...]]
    row, col = square_indices(step)
    diagonals, norm_sq = [None] * PACK, 0.0
    for half, first, second in zip(halves, (0, 1), (3, 2)):
        block = half[:step, :step]
        upper, lower = jnp.where(row < col, block, 0.0), jnp.where(row > col, block, 0.0)
        one = jnp.where(row == col, block, 0.0)
        two = jnp.where(row == col, half[step : step + 1, :step], 0.0)
        both = jnp.sum(one + two, axis=1, keepdims=True)
        norm_sq = norm_sq + jnp.sum(both, axis=0, keepdims=True)
        diagonals[first] = upper + upper.T + one
        diagonals[second] = lower + lower.T + two
    factor = 1.0 / (jnp.sqrt(norm_sq) + norm_epsilon)
    square = factor * factor
    middle = [(PACK - i) * step for i in range(PACK)]
    bands = [
        halves[0][:step, step : middle[0]],
        halves[1][:step, step : middle[1]],
        halves[1][:step, middle[1] :],
    ]
    for i, diagonal in enumerate(diagonals):
        gram[i * step : (i + 1) * step, i * step : (i + 1) * step] = diagonal * square
    for i, band in enumerate(bands):
        scaled = band * square
        gram[i * step : (i + 1) * step, (i + 1) * step :] = scaled
        for j in range(i + 1, PACK):
            gram[j * step : (j + 1) * step, i * step : (i + 1) * step] = scaled[
                :, (j - i - 1) * step : (j - i) * step
            ].T
    cur[...] = p_ref[...] * factor

    def mixed_of(a, a_parts):
        return second_coeff * a + third_coeff * even_product(a_parts[:2], a_parts[:2])

    def apply(mixed_parts):
        x = cur[...]
        return first_coeff * x + split_product(mixed_parts[:2], parts_of(x, 2))

    def advance(count):
        a = gram[...]
        a_parts = parts_of(a, count)
        mixed_parts = parts_of(mixed_of(a, a_parts if count == 2 else parts_of(a, 2)), count)
        half_way = first_coeff * a + even_product(mixed_parts, a_parts)
        gram[...] = first_coeff * half_way + even_product(
            parts_of(half_way, count), mixed_parts
        )
        cur[...] = apply(mixed_parts)

    advance(3)
    if iters > 2:
        lax.fori_loop(1, iters - 1, lambda _, none: (advance(2), none)[1], 0)
    a = gram[...]
    u = apply(parts_of(mixed_of(a, parts_of(a, 2)), 2)) * scale
    w = w_ref[...]
    new = w - learn_rate * (u + weight_decay * w)
    rounded = new.astype(r_ref.dtype)
    r_ref[...] = rounded
    for i, piece in enumerate(pieces):
        piece[...] = rounded[i * piece.shape[0] : (i + 1) * piece.shape[0]]
    u_ref[...] = u


def newton(halves, moved, nesterov, master, iters, scale, chunks):
    rows, cols = nesterov.shape
    vmem = pl.BlockSpec(memory_space=pltpu.VMEM)
    f32 = jax.ShapeDtypeStruct((rows, cols), jnp.float32)
    pieces = [jax.ShapeDtypeStruct((rows // chunks, cols), jnp.bfloat16) for _ in range(chunks)]
    return pl.pallas_call(
        functools.partial(newton_kernel, iters, scale),
        out_shape=[f32, jax.ShapeDtypeStruct((rows, cols), jnp.bfloat16)] + pieces,
        in_specs=[vmem] * 6,
        out_specs=[vmem] * (2 + chunks),
        scratch_shapes=[
            pltpu.VMEM((rows, rows), jnp.float32),
            pltpu.VMEM((rows, cols), jnp.float32),
        ],
        cost_estimate=pl.CostEstimate(
            flops=2 * 60 * rows * rows * cols, bytes_accessed=24 * rows * cols, transcendentals=0
        ),
        compiler_params=pltpu.CompilerParams(vmem_limit_bytes=24 << 20),
    )(halves[0], moved[0], halves[1], moved[1], nesterov, master)


def flipped(block, axis, flip):
    return lax.ppermute(block, axis, [(i, i ^ flip) for i in range(lax.axis_size(axis))])


def owner_of(owned_matrix, quads):
    ids = jnp.arange(quads, dtype=jnp.int32)
    return jnp.sum(
        jnp.where(owned_matrix[:, :, None] == ids[None, None, :], ids[None, :, None], 0), axis=1
    ).reshape(-1)


def wanted_slots(rollout_matrix, owned_matrix, share_count):
    quads = owned_matrix.shape[1]
    group = lax.axis_index("grp")
    place = lax.axis_index("dev")
    inverse = owner_of(owned_matrix, quads)
    mats = jnp.arange(inverse.shape[0], dtype=jnp.int32)
    targets = rollout_matrix[0]
    owner = jnp.sum(jnp.where(targets[:, None] == mats[None, :], inverse[None, :], 0), axis=1)
    slot = ((targets // quads) ^ group) * quads + (owner ^ (place // share_count))
    turns = place ^ jnp.arange(share_count, dtype=jnp.int32)
    places = jnp.arange(slot.shape[0], dtype=jnp.int32)
    return jnp.sum(jnp.where(turns[:, None] == places[None, :], slot[None, :], 0), axis=1)


def pick_kernel(chunk, slots, *refs):
    turns = slots.shape[0]
    slabs, outs, done = refs[: -turns - 1], refs[-turns - 1 : -1], refs[-1]
    rows = outs[0].shape[0]
    views = [
        slab if slab.shape[0] == rows else slab.at[pl.ds(chunk * rows, rows)] for slab in slabs
    ]
    for turn in range(turns):
        slot = slots[turn]
        for index, view in enumerate(views):

            @pl.when(slot == index)
            def _(view=view, turn=turn):
                pltpu.make_async_copy(view, outs[turn], done.at[turn]).start()

    for turn in range(turns):
        pltpu.make_async_copy(views[0], outs[turn], done.at[turn]).wait()


def pick(slots, slabs, chunk, rows):
    turns = slots.shape[0]
    cols = slabs[0].shape[1]
    block = jax.ShapeDtypeStruct((rows, cols), slabs[0].dtype)
    return pl.pallas_call(
        functools.partial(pick_kernel, chunk),
        out_shape=[block] * turns,
        in_specs=[pl.BlockSpec(memory_space=pltpu.SMEM)]
        + [pl.BlockSpec(memory_space=pl.ANY)] * len(slabs),
        out_specs=[pl.BlockSpec(memory_space=pltpu.VMEM)] * turns,
        scratch_shapes=[pltpu.SemaphoreType.DMA((turns,))],
        cost_estimate=pl.CostEstimate(
            flops=0, bytes_accessed=4 * turns * rows * cols, transcendentals=0
        ),
        compiler_params=pltpu.CompilerParams(vmem_limit_bytes=8 << 20),
    )(slots, *slabs)


def lay_kernel(share_count, chunk, *refs):
    mine = lax.axis_index("dev") % share_count
    blocks, out, done = refs[:share_count], refs[-2], refs[-1]
    rows, cols = blocks[0].shape
    moves = []
    for turn, block in enumerate(blocks):
        start = pl.multiple_of((mine ^ turn) * cols, cols)
        place = out.at[pl.ds(chunk * rows, rows), pl.ds(start, cols)]
        moves.append(pltpu.make_async_copy(block, place, done.at[turn]))
    for move in moves:
        move.start()
    for move in moves:
        move.wait()


def lay(blocks, chunk, chunks, before):
    share_count = len(blocks)
    rows, cols = blocks[0].shape
    extra = [] if before is None else [before]
    return pl.pallas_call(
        functools.partial(lay_kernel, share_count, chunk),
        out_shape=jax.ShapeDtypeStruct((rows * chunks, cols * share_count), blocks[0].dtype),
        in_specs=[pl.BlockSpec(memory_space=pltpu.VMEM)] * share_count
        + [pl.BlockSpec(memory_space=pltpu.HBM)] * len(extra),
        out_specs=pl.BlockSpec(memory_space=pltpu.HBM),
        scratch_shapes=[pltpu.SemaphoreType.DMA((share_count,))],
        input_output_aliases={share_count: 0} if extra else {},
        cost_estimate=pl.CostEstimate(
            flops=0, bytes_accessed=4 * share_count * rows * cols, transcendentals=0
        ),
        compiler_params=pltpu.CompilerParams(vmem_limit_bytes=8 << 20),
    )(*blocks, *extra)


def spread(block):
    group_count = lax.axis_size("grp")
    table = {0: block}
    for bit in range(group_count.bit_length() - 2, -1, -1):
        for key in list(table):
            table[key | 1 << bit] = flipped(table[key], "grp", 1 << bit)
    return [table[key] for key in range(group_count)]


def sync_two_halves(rounded, pieces, slots, share_count):
    chunks = len(pieces)
    rows = pieces[0].shape[0]
    others = []
    for piece in pieces:
        others.append(flipped(piece, "dev", share_count))
    mine = spread(rounded)
    result = None
    for chunk in range(chunks):
        theirs = spread(others[chunk])
        slabs = [slab for pair in zip(mine, theirs) for slab in pair]
        blocks = list(pick(slots, slabs, chunk, rows))
        for turn in range(1, share_count):
            blocks[turn] = flipped(blocks[turn], "dev", turn)
        result = lay(blocks, chunk, chunks, result)
    return result


def sync_any(rounded, rollout_matrix, owned_matrix, row_block, columns):
    dev_count = lax.axis_size("dev")
    group_count = lax.axis_size("grp")
    quads = owned_matrix.shape[1]
    row_count, slab_cols = rounded.shape
    all_mats = group_count * quads
    slot_count = all_mats // dev_count
    own_rows = lax.all_to_all(
        rounded.reshape(dev_count, row_block, slab_cols),
        "dev",
        split_axis=0,
        concat_axis=2,
        tiled=True,
    )
    copies = lax.all_gather(own_rows, "grp", axis=0, tiled=True)
    blocks = copies.reshape(group_count, row_block, quads, columns)
    inverse_flat = owner_of(owned_matrix, quads)
    targets = rollout_matrix[0]
    global_ids = jnp.arange(all_mats, dtype=jnp.int32)
    target_group = targets // quads
    target_owner = jnp.sum(
        jnp.where(targets[:, None] == global_ids[None, :], inverse_flat[None, :], 0), axis=1
    )
    flat_owner = target_group * quads + target_owner
    chooser = (
        (flat_owner[:, None] == global_ids[None, :])
        .astype(jnp.bfloat16)
        .reshape(all_mats, group_count, quads)
    )
    outgoing = jnp.einsum(
        "pgq,grqc->prc", chooser, blocks, preferred_element_type=jnp.float32
    ).astype(jnp.bfloat16)
    landed = lax.all_to_all(
        outgoing.reshape(dev_count, slot_count, row_block, columns),
        "dev",
        split_axis=0,
        concat_axis=2,
        tiled=True,
    )
    return landed.reshape(slot_count, row_count, columns)


def step(gradient, momentum, master_weight, owned_matrix, rollout_matrix):
    group = lax.axis_index("grp")
    dev_count = lax.axis_size("dev")
    group_count = lax.axis_size("grp")
    quads = gradient.shape[0]
    row_block = gradient.shape[1]
    columns = gradient.shape[2]
    slab_cols = momentum.shape[2]
    row_count = momentum.shape[1]
    share_count = columns // slab_cols
    two_halves = (
        quads == 2
        and dev_count == quads * share_count
        and not share_count & (share_count - 1)
        and not group_count & (group_count - 1)
    )
    two_halves = (
        quads == 2
        and dev_count == quads * share_count
        and not share_count & (share_count - 1)
        and not group_count & (group_count - 1)
    )
    if two_halves:
        dealt = list(deal(gradient, owned_matrix, share_count))
        for turn in [*range(share_count, dev_count), *range(1, share_count)]:
            dealt[turn] = flipped(dealt[turn], "dev", turn)
        slots = wanted_slots(rollout_matrix, owned_matrix, share_count)
    else:
        mine = lax.dynamic_index_in_dim(owned_matrix, group, 0, keepdims=False)
        local_ids = jnp.arange(quads, dtype=jnp.int32)
        picker = (mine[:, None] == local_ids[None, :]).astype(jnp.bfloat16)
        ordered = jnp.einsum(
            "qm,mrc->rqc", picker, gradient, preferred_element_type=jnp.float32
        ).astype(jnp.bfloat16)
        arrived = lax.all_to_all(
            ordered.reshape(row_block, dev_count, slab_cols),
            "dev",
            split_axis=1,
            concat_axis=0,
            tiled=True,
        )
        dealt = [arrived.reshape(row_count, slab_cols)]
    new_moment, nesterov, *halves = gram_halves(momentum[0], dealt)
    if two_halves:
        halves, slots = lax.optimization_barrier((halves, slots))
    halves, moved = gram_sum(halves, share_count)
    scale_factor = 0.2 * math.sqrt(max(row_count, columns))
    update, rounded, *pieces = newton(
        halves, moved, nesterov, master_weight[0], ITERS, scale_factor, CHUNKS if two_halves else 0
    )
    master = master_weight[0]
    new_weight = master - learn_rate * (update + weight_decay * master)
    if two_halves:
        rollout = sync_two_halves(rounded, pieces, slots, share_count)[None]
    else:
        rollout = sync_any(rounded, rollout_matrix, owned_matrix, row_block, columns)
    return (new_moment[None], update[None], new_weight[None], rollout)


def solution(mesh):
    placed = (
        P("grp", "dev", None),
        P(("grp", "dev"), None, None),
        P(("grp", "dev"), None, None),
        P(),
        P("grp", None),
    )
    return jax.shard_map(
        step,
        mesh=mesh,
        in_specs=placed,
        out_specs=(
            P(("grp", "dev"), None, None),
            P(("grp", "dev"), None, None),
            P(("grp", "dev"), None, None),
            P(("grp", "dev"), None, None),
        ),
        check_vma=False,
    )
```

```python
import functools
import math

import jax
import jax.numpy as jnp
from jax import lax
from jax.experimental import pallas as pl
from jax.experimental.pallas import tpu as pltpu
from jax.sharding import PartitionSpec as P


ITERS = 5
PACK = 4
STRIP = 8
CHUNKS = 2


momentum_decay = 0.95
learn_rate = 0.02
weight_decay = 0.1
first_coeff = 3.4445
second_coeff = -4.775
third_coeff = 2.0315
norm_epsilon = 1e-07


def from_partner(block, axis, bit):
    count = lax.axis_size(axis)
    route = []
    for low in range(count):
        high = low | 1 << bit
        if high != low and high < count:
            route += [(low, high), (high, low)]
    return lax.ppermute(block, axis, route)


def parts_of(value, count):
    parts = []
    for _ in range(count - 1):
        high = value.astype(jnp.bfloat16)
        parts.append(high)
        value = value - high.astype(jnp.float32)
    return parts + [value.astype(jnp.bfloat16)]


def square_indices(size):
    return [lax.broadcasted_iota(jnp.int32, (size, size), axis) for axis in range(2)]


def split_product(left, right, turned=False):
    count = len(left)
    terms = [(i, order - i) for order in range(count - 1, -1, -1) for i in range(order + 1)]
    axis = 1 if turned else 0
    return lax.dot_general(
        jnp.concatenate([left[i] for i, _ in terms], axis=1),
        jnp.concatenate([right[j] for _, j in terms], axis=axis),
        (((1,), (axis,)), ((), ())),
        preferred_element_type=jnp.float32,
    )


def even_product(left, right):
    half = left[0].shape[0] // 2
    top = split_product([part[:half] for part in left], right)
    low = split_product([part[half:] for part in left], [part[:, half:] for part in right])
    bottom = jnp.concatenate([top[:, half:].T, low], axis=1)
    return jnp.concatenate([top, bottom], axis=0)


def deal_kernel(share_count, owned, gradient, *refs):
    outs, done = refs[:-1], refs[-1]
    group = lax.axis_index("grp")
    place = lax.axis_index("dev")
    cols = outs[0].shape[1]
    moves = []
    for turn, out in enumerate(outs):
        target = place ^ turn
        column = pl.multiple_of((target % share_count) * cols, cols)
        block = gradient.at[owned[target // share_count, group], :, pl.ds(column, cols)]
        moves.append(pltpu.make_async_copy(block, out, done.at[turn]))
    for move in moves:
        move.start()
    for move in moves:
        move.wait()


def deal(gradient, owned_matrix, share_count):
    quads, rows, columns = gradient.shape
    turns = quads * share_count
    block = jax.ShapeDtypeStruct((rows, columns // share_count), gradient.dtype)
    return pl.pallas_call(
        functools.partial(deal_kernel, share_count),
        out_shape=[block] * turns,
        in_specs=[pl.BlockSpec(memory_space=pltpu.SMEM), pl.BlockSpec(memory_space=pl.ANY)],
        out_specs=[pl.BlockSpec(memory_space=pltpu.VMEM)] * turns,
        scratch_shapes=[pltpu.SemaphoreType.DMA((turns,))],
        cost_estimate=pl.CostEstimate(
            flops=0, bytes_accessed=4 * gradient.size, transcendentals=0
        ),
        compiler_params=pltpu.CompilerParams(vmem_limit_bytes=8 << 20),
    )(owned_matrix.T, gradient)


def gram_kernel(m_ref, *refs):
    blocks, (nm_ref, p_ref, a_ref, b_ref) = refs[:-4], refs[-4:]
    place = lax.axis_index("dev") if len(blocks) > 1 else 0
    for turn, block in enumerate(blocks):
        size = block.shape[0]
        rows = pl.ds(pl.multiple_of((place ^ turn) * size, size), size)
        grad = block[...].astype(jnp.float32)
        moment = momentum_decay * m_ref[rows, :] + grad
        nm_ref[rows, :] = moment
        p_ref[rows, :] = grad + momentum_decay * moment
    parts = parts_of(p_ref[...], 3)
    step = p_ref.shape[0] // PACK
    row, col = square_indices(step)

    def band(i):
        low = i * step
        return split_product(
            [part[low : low + step] for part in parts], [part[low:] for part in parts], turned=True
        )

    for ref, first, second in ((a_ref, 0, 3), (b_ref, 1, 2)):
        one, two = band(first), band(second)
        ref[:step, :step] = jnp.where(row <= col, one[:, :step], two[:, :step])
        middle = (PACK - first) * step
        ref[:step, step:middle] = one[:, step:]
        if second < PACK - 1:
            ref[:step, middle:] = two[:, step:]
        ref[step:, :] = jnp.zeros((STRIP, ref.shape[1]), jnp.float32)
        diagonal = jnp.sum(jnp.where(row == col, two[:, :step], 0.0), axis=0, keepdims=True)
        ref[step:, :step] = jnp.broadcast_to(diagonal, (STRIP, step))


def gram_halves(momentum, blocks):
    rows, cols = momentum.shape
    vmem = pl.BlockSpec(memory_space=pltpu.VMEM)
    f32 = jax.ShapeDtypeStruct((rows, cols), jnp.float32)
    half = jax.ShapeDtypeStruct((rows // PACK + STRIP, rows), jnp.float32)
    return pl.pallas_call(
        gram_kernel,
        out_shape=[f32, f32, half, half],
        in_specs=[vmem] * (1 + len(blocks)),
        out_specs=[vmem] * 4,
        cost_estimate=pl.CostEstimate(
            flops=8 * rows * rows * cols, bytes_accessed=16 * rows * cols, transcendentals=0
        ),
        compiler_params=pltpu.CompilerParams(vmem_limit_bytes=24 << 20),
    )(momentum, *blocks)


def gram_sum(halves, share_count):
    moved = [jnp.zeros_like(half) for half in halves]
    bits = list(range(share_count.bit_length() - 1))
    orders = [bits, bits[::-1]]
    for turn in range(len(bits)):
        halves = [half + other for half, other in zip(halves, moved)] if turn else halves
        moved = [from_partner(half, "dev", order[turn]) for half, order in zip(halves, orders)]
    return halves, moved


def newton_kernel(iters, scale, a0, a1, b0, b1, p_ref, w_ref, u_ref, r_ref, *rest):
    pieces, (gram, cur) = rest[:-2], rest[-2:]
    rows = gram.shape[0]
    step = rows // PACK
    halves = [a0[...] + a1[...], b0[...] + b1[...]]
    row, col = square_indices(step)
    diagonals, norm_sq = [None] * PACK, 0.0
    for half, first, second in zip(halves, (0, 1), (3, 2)):
        block = half[:step, :step]
        upper, lower = jnp.where(row < col, block, 0.0), jnp.where(row > col, block, 0.0)
        one = jnp.where(row == col, block, 0.0)
        two = jnp.where(row == col, half[step : step + 1, :step], 0.0)
        both = jnp.sum(one + two, axis=1, keepdims=True)
        norm_sq = norm_sq + jnp.sum(both, axis=0, keepdims=True)
        diagonals[first] = upper + upper.T + one
        diagonals[second] = lower + lower.T + two
    factor = 1.0 / (jnp.sqrt(norm_sq) + norm_epsilon)
    square = factor * factor
    middle = [(PACK - i) * step for i in range(PACK)]
    bands = [
        halves[0][:step, step : middle[0]],
        halves[1][:step, step : middle[1]],
        halves[1][:step, middle[1] :],
    ]
    for i, diagonal in enumerate(diagonals):
        gram[i * step : (i + 1) * step, i * step : (i + 1) * step] = diagonal * square
    for i, band in enumerate(bands):
        scaled = band * square
        gram[i * step : (i + 1) * step, (i + 1) * step :] = scaled
        for j in range(i + 1, PACK):
            gram[j * step : (j + 1) * step, i * step : (i + 1) * step] = scaled[
                :, (j - i - 1) * step : (j - i) * step
            ].T
    cur[...] = p_ref[...] * factor

    def mixed_of(a, a_parts):
        return second_coeff * a + third_coeff * even_product(a_parts[:2], a_parts[:2])

    def apply(mixed_parts):
        x = cur[...]
        return first_coeff * x + split_product(mixed_parts[:2], parts_of(x, 2))

    def advance(count):
        a = gram[...]
        a_parts = parts_of(a, count)
        mixed_parts = parts_of(mixed_of(a, a_parts), count)
        half_way = first_coeff * a + even_product(mixed_parts, a_parts)
        gram[...] = first_coeff * half_way + even_product(
            parts_of(half_way, count), mixed_parts
        )
        cur[...] = apply(mixed_parts)

    advance(3)
    if iters > 2:
        lax.fori_loop(1, iters - 1, lambda _, none: (advance(2), none)[1], 0)
    a = gram[...]
    u = apply(parts_of(mixed_of(a, parts_of(a, 2)), 2)) * scale
    w = w_ref[...]
    new = w - learn_rate * (u + weight_decay * w)
    rounded = new.astype(r_ref.dtype)
    r_ref[...] = rounded
    for i, piece in enumerate(pieces):
        piece[...] = rounded[i * piece.shape[0] : (i + 1) * piece.shape[0]]
    u_ref[...] = u


def newton(halves, moved, nesterov, master, iters, scale, chunks):
    rows, cols = nesterov.shape
    vmem = pl.BlockSpec(memory_space=pltpu.VMEM)
    f32 = jax.ShapeDtypeStruct((rows, cols), jnp.float32)
    pieces = [jax.ShapeDtypeStruct((rows // chunks, cols), jnp.bfloat16) for _ in range(chunks)]
    return pl.pallas_call(
        functools.partial(newton_kernel, iters, scale),
        out_shape=[f32, jax.ShapeDtypeStruct((rows, cols), jnp.bfloat16)] + pieces,
        in_specs=[vmem] * 6,
        out_specs=[vmem] * (2 + chunks),
        scratch_shapes=[
            pltpu.VMEM((rows, rows), jnp.float32),
            pltpu.VMEM((rows, cols), jnp.float32),
        ],
        cost_estimate=pl.CostEstimate(
            flops=2 * 60 * rows * rows * cols, bytes_accessed=24 * rows * cols, transcendentals=0
        ),
        compiler_params=pltpu.CompilerParams(vmem_limit_bytes=24 << 20),
    )(halves[0], moved[0], halves[1], moved[1], nesterov, master)


def flipped(block, axis, flip):
    return lax.ppermute(block, axis, [(i, i ^ flip) for i in range(lax.axis_size(axis))])


def owner_of(owned_matrix, quads):
    ids = jnp.arange(quads, dtype=jnp.int32)
    return jnp.sum(
        jnp.where(owned_matrix[:, :, None] == ids[None, None, :], ids[None, :, None], 0), axis=1
    ).reshape(-1)


def wanted_slots(rollout_matrix, owned_matrix, share_count):
    quads = owned_matrix.shape[1]
    group = lax.axis_index("grp")
    place = lax.axis_index("dev")
    inverse = owner_of(owned_matrix, quads)
    mats = jnp.arange(inverse.shape[0], dtype=jnp.int32)
    targets = rollout_matrix[0]
    owner = jnp.sum(jnp.where(targets[:, None] == mats[None, :], inverse[None, :], 0), axis=1)
    slot = ((targets // quads) ^ group) * quads + (owner ^ (place // share_count))
    turns = place ^ jnp.arange(share_count, dtype=jnp.int32)
    places = jnp.arange(slot.shape[0], dtype=jnp.int32)
    return jnp.sum(jnp.where(turns[:, None] == places[None, :], slot[None, :], 0), axis=1)


def pick_kernel(chunk, slots, *refs):
    turns = slots.shape[0]
    slabs, outs, done = refs[: -turns - 1], refs[-turns - 1 : -1], refs[-1]
    rows = outs[0].shape[0]
    views = [
        slab if slab.shape[0] == rows else slab.at[pl.ds(chunk * rows, rows)] for slab in slabs
    ]
    for turn in range(turns):
        slot = slots[turn]
        for index, view in enumerate(views):

            @pl.when(slot == index)
            def _(view=view, turn=turn):
                pltpu.make_async_copy(view, outs[turn], done.at[turn]).start()

    for turn in range(turns):
        pltpu.make_async_copy(views[0], outs[turn], done.at[turn]).wait()


def pick(slots, slabs, chunk, rows):
    turns = slots.shape[0]
    cols = slabs[0].shape[1]
    block = jax.ShapeDtypeStruct((rows, cols), slabs[0].dtype)
    return pl.pallas_call(
        functools.partial(pick_kernel, chunk),
        out_shape=[block] * turns,
        in_specs=[pl.BlockSpec(memory_space=pltpu.SMEM)]
        + [pl.BlockSpec(memory_space=pl.ANY)] * len(slabs),
        out_specs=[pl.BlockSpec(memory_space=pltpu.VMEM)] * turns,
        scratch_shapes=[pltpu.SemaphoreType.DMA((turns,))],
        cost_estimate=pl.CostEstimate(
            flops=0, bytes_accessed=4 * turns * rows * cols, transcendentals=0
        ),
        compiler_params=pltpu.CompilerParams(vmem_limit_bytes=8 << 20),
    )(slots, *slabs)


def lay_kernel(share_count, chunk, *refs):
    mine = lax.axis_index("dev") % share_count
    blocks, out, done = refs[:share_count], refs[-2], refs[-1]
    rows, cols = blocks[0].shape
    moves = []
    for turn, block in enumerate(blocks):
        start = pl.multiple_of((mine ^ turn) * cols, cols)
        place = out.at[pl.ds(chunk * rows, rows), pl.ds(start, cols)]
        moves.append(pltpu.make_async_copy(block, place, done.at[turn]))
    for move in moves:
        move.start()
    for move in moves:
        move.wait()


def lay(blocks, chunk, chunks, before):
    share_count = len(blocks)
    rows, cols = blocks[0].shape
    extra = [] if before is None else [before]
    return pl.pallas_call(
        functools.partial(lay_kernel, share_count, chunk),
        out_shape=jax.ShapeDtypeStruct((rows * chunks, cols * share_count), blocks[0].dtype),
        in_specs=[pl.BlockSpec(memory_space=pltpu.VMEM)] * share_count
        + [pl.BlockSpec(memory_space=pltpu.HBM)] * len(extra),
        out_specs=pl.BlockSpec(memory_space=pltpu.HBM),
        scratch_shapes=[pltpu.SemaphoreType.DMA((share_count,))],
        input_output_aliases={share_count: 0} if extra else {},
        cost_estimate=pl.CostEstimate(
            flops=0, bytes_accessed=4 * share_count * rows * cols, transcendentals=0
        ),
        compiler_params=pltpu.CompilerParams(vmem_limit_bytes=8 << 20),
    )(*blocks, *extra)


def spread(block):
    group_count = lax.axis_size("grp")
    table = {0: block}
    for bit in range(group_count.bit_length() - 2, -1, -1):
        for key in list(table):
            table[key | 1 << bit] = flipped(table[key], "grp", 1 << bit)
    return [table[key] for key in range(group_count)]


def sync_two_halves(rounded, pieces, slots, share_count):
    chunks = len(pieces)
    rows = pieces[0].shape[0]
    others = []
    for piece in pieces:
        others.append(flipped(piece, "dev", share_count))
    mine = spread(rounded)
    result = None
    for chunk in range(chunks):
        theirs = spread(others[chunk])
        slabs = [slab for pair in zip(mine, theirs) for slab in pair]
        blocks = list(pick(slots, slabs, chunk, rows))
        for turn in range(1, share_count):
            blocks[turn] = flipped(blocks[turn], "dev", turn)
        result = lay(blocks, chunk, chunks, result)
    return result


def sync_any(rounded, rollout_matrix, owned_matrix, row_block, columns):
    dev_count = lax.axis_size("dev")
    group_count = lax.axis_size("grp")
    quads = owned_matrix.shape[1]
    row_count, slab_cols = rounded.shape
    all_mats = group_count * quads
    slot_count = all_mats // dev_count
    own_rows = lax.all_to_all(
        rounded.reshape(dev_count, row_block, slab_cols),
        "dev",
        split_axis=0,
        concat_axis=2,
        tiled=True,
    )
    copies = lax.all_gather(own_rows, "grp", axis=0, tiled=True)
    blocks = copies.reshape(group_count, row_block, quads, columns)
    inverse_flat = owner_of(owned_matrix, quads)
    targets = rollout_matrix[0]
    global_ids = jnp.arange(all_mats, dtype=jnp.int32)
    target_group = targets // quads
    target_owner = jnp.sum(
        jnp.where(targets[:, None] == global_ids[None, :], inverse_flat[None, :], 0), axis=1
    )
    flat_owner = target_group * quads + target_owner
    chooser = (
        (flat_owner[:, None] == global_ids[None, :])
        .astype(jnp.bfloat16)
        .reshape(all_mats, group_count, quads)
    )
    outgoing = jnp.einsum(
        "pgq,grqc->prc", chooser, blocks, preferred_element_type=jnp.float32
    ).astype(jnp.bfloat16)
    landed = lax.all_to_all(
        outgoing.reshape(dev_count, slot_count, row_block, columns),
        "dev",
        split_axis=0,
        concat_axis=2,
        tiled=True,
    )
    return landed.reshape(slot_count, row_count, columns)


def step(gradient, momentum, master_weight, owned_matrix, rollout_matrix):
    group = lax.axis_index("grp")
    dev_count = lax.axis_size("dev")
    group_count = lax.axis_size("grp")
    quads = gradient.shape[0]
    row_block = gradient.shape[1]
    columns = gradient.shape[2]
    slab_cols = momentum.shape[2]
    row_count = momentum.shape[1]
    share_count = columns // slab_cols
    two_halves = (
        quads == 2
        and dev_count == quads * share_count
        and not share_count & (share_count - 1)
        and not group_count & (group_count - 1)
    )
    two_halves = (
        quads == 2
        and dev_count == quads * share_count
        and not share_count & (share_count - 1)
        and not group_count & (group_count - 1)
    )
    if two_halves:
        dealt = list(deal(gradient, owned_matrix, share_count))
        for turn in [*range(share_count, dev_count), *range(1, share_count)]:
            dealt[turn] = flipped(dealt[turn], "dev", turn)
        slots = wanted_slots(rollout_matrix, owned_matrix, share_count)
    else:
        mine = lax.dynamic_index_in_dim(owned_matrix, group, 0, keepdims=False)
        local_ids = jnp.arange(quads, dtype=jnp.int32)
        picker = (mine[:, None] == local_ids[None, :]).astype(jnp.bfloat16)
        ordered = jnp.einsum(
            "qm,mrc->rqc", picker, gradient, preferred_element_type=jnp.float32
        ).astype(jnp.bfloat16)
        arrived = lax.all_to_all(
            ordered.reshape(row_block, dev_count, slab_cols),
            "dev",
            split_axis=1,
            concat_axis=0,
            tiled=True,
        )
        dealt = [arrived.reshape(row_count, slab_cols)]
    new_moment, nesterov, *halves = gram_halves(momentum[0], dealt)
    if two_halves:
        halves, slots = lax.optimization_barrier((halves, slots))
    halves, moved = gram_sum(halves, share_count)
    scale_factor = 0.2 * math.sqrt(max(row_count, columns))
    update, rounded, *pieces = newton(
        halves, moved, nesterov, master_weight[0], ITERS, scale_factor, CHUNKS if two_halves else 0
    )
    master = master_weight[0]
    new_weight = master - learn_rate * (update + weight_decay * master)
    if two_halves:
        rollout = sync_two_halves(rounded, pieces, slots, share_count)[None]
    else:
        rollout = sync_any(rounded, rollout_matrix, owned_matrix, row_block, columns)
    return (new_moment[None], update[None], new_weight[None], rollout)


def solution(mesh):
    placed = (
        P("grp", "dev", None),
        P(("grp", "dev"), None, None),
        P(("grp", "dev"), None, None),
        P(),
        P("grp", None),
    )
    return jax.shard_map(
        step,
        mesh=mesh,
        in_specs=placed,
        out_specs=(
            P(("grp", "dev"), None, None),
            P(("grp", "dev"), None, None),
            P(("grp", "dev"), None, None),
            P(("grp", "dev"), None, None),
        ),
        check_vma=False,
    )
```
